32 devices in a mesh: cube: 2 (over core), row: 4 (over y, x), col: 4 (over z).
Axes of the slice: x: 2, y: 2, z: 4, core: 2. Of those that a mesh axis runs over, the one named last changes fastest.
Arguments:
- child_update: float32 [2, 8192, 8192], P('cube', 'row', 'col'), may hold values from -8 to 80, as said below
- child_panel: bfloat16 [2, 8192, 2048], P('cube', 'row'), may hold values from -8 to 8
- parent_front: bfloat16 [16384, 16384], P('row', ('cube', 'col')), may hold values from -8 to 520, as said below
- block_map: int32 [2, 64], replicated, may hold values from 0 to 127, as said below
Outputs:
- schur: float32 [16384, 16384], P('row', ('cube', 'col'))
- panel: float32 [16384, 512], P('row')
The draws below stay inside these ranges and needn't reach their ends.
Inputs may be any that keep to these rules, and one draw needn't show every extreme that they name: child_update[k] is symmetric for every child. parent_front is symmetric, and the leading 512 x 512 block of front is positive definite. `block_map`: for each child the 64 entries are distinct. Split a child's entries into aligned groups of 16 entries. In every group, for each r from 0 to 3, exactly 4 entries e have e // 32 equal to r. In every group, at most 2 entries share one value of e // 16, and every group has a value shared by 2 entries.
All inputs are finite; a program needn't handle non-finite values.
Results may differ from the reference program's by a relative error of at most 0.00044.
Values may be sent and summed in bfloat16 or wider, within the bound.
A program may use at most 320 MiB of HBM per device.

```python
import math
import jax
import jax.numpy as jnp

CONTRIB = 8192
PARENT = 16384
BLK = 128
PANEL = 512
KW = 2048
CHILDREN = 2
CHILD_BLOCKS = 64
PARENT_BLOCKS = 128


fine_rows = 8


fine_cols = 16


def panel_fan():
    return max(1, KW // 64)


def draw_child_panel(key, part):
    shape_all = (CHILDREN, CONTRIB, KW)
    spread = 1.0 / math.sqrt(panel_fan())
    raw_draw = jnp.clip(jax.random.normal(key, shape_all, jnp.float32), -6.0, 6.0)
    return (raw_draw * spread).astype(jnp.bfloat16)


def draw_child_update(key, part):
    shape_all = (CHILDREN, CONTRIB, CONTRIB)
    raw_draw = jnp.clip(jax.random.normal(key, shape_all, jnp.float32), -5.6, 5.6)
    symmetric = (raw_draw + jnp.swapaxes(raw_draw, 1, 2)) * 0.7071
    base_shift = float(KW // panel_fan())
    shifts = jax.random.uniform(jax.random.fold_in(key, 11), (CHILDREN, CONTRIB), jnp.float32, base_shift + 2.0, base_shift + 8.0)
    indices = jnp.arange(CONTRIB)
    symmetric = symmetric.at[:, indices, indices].add(shifts)
    return symmetric.astype(jnp.float32)


def draw_parent_front(key, part):
    shape_pair = (PARENT, PARENT)
    raw_draw = jnp.clip(jax.random.normal(key, shape_pair, jnp.float32), -5.6, 5.6)
    symmetric = (raw_draw + raw_draw.T) * 0.7071
    pivot_low = 2 * (KW + 2 * PANEL) // panel_fan() + PANEL // 4 + 16
    pivot_high = pivot_low + pivot_low // 2
    pivot_part = jax.random.uniform(jax.random.fold_in(key, 7), (PARENT,), jnp.float32, float(pivot_low), float(pivot_high))
    other_part = jax.random.uniform(jax.random.fold_in(key, 9), (PARENT,), jnp.float32, 4.0, 12.0)
    indices = jnp.arange(PARENT)
    diagonal = jnp.where(indices < PANEL, pivot_part, other_part)
    symmetric = symmetric.at[indices, indices].add(diagonal)
    return symmetric.astype(jnp.bfloat16)


def child_map(key):
    total_blocks = CONTRIB // BLK
    parent_blocks = PARENT // BLK
    group_size = total_blocks // fine_rows
    group_count = total_blocks // group_size
    span_cols = parent_blocks // fine_cols
    split_keys = jax.random.split(key, 3)
    group_ids = jnp.arange(group_count, dtype=jnp.int32)[:, None]
    member_ids = jnp.arange(group_size, dtype=jnp.int32)[None, :]
    row_range = jnp.broadcast_to(member_ids % fine_rows, (group_count, group_size))
    flip_bits = jax.random.randint(split_keys[0], (group_count, group_size), 0, 2, dtype=jnp.int32)
    column_range = 2 * row_range + flip_bits
    offset_rank = jnp.broadcast_to(group_ids, (group_count, group_size))
    orders = jax.vmap(lambda sub_key: jax.random.permutation(sub_key, span_cols))(jax.random.split(split_keys[1], fine_cols))
    position = orders[column_range, offset_rank]
    target = span_cols * column_range + position
    shuffles = jax.vmap(lambda sub_key: jax.random.permutation(sub_key, group_size))(jax.random.split(split_keys[2], group_count))
    mapped = jnp.take_along_axis(target, shuffles, axis=1)
    return mapped.reshape(total_blocks).astype(jnp.int32)


def draw_block_map(key, part):
    return jax.vmap(child_map)(jax.random.split(key, CHILDREN)).astype(jnp.int32)


def setup_inputs(seed: int = 0) -> dict:
    streams_of = jax.random.split(jax.random.key(seed), 5)
    return {
        "child_update": draw_child_update(jax.random.fold_in(streams_of[4], 71), 0),
        "child_panel": draw_child_panel(jax.random.fold_in(streams_of[4], 71), 0),
        "parent_front": draw_parent_front(jax.random.fold_in(streams_of[4], 71), 0),
        "block_map": draw_block_map(jax.random.fold_in(streams_of[4], 71), 0),
    }


def reference(child_update, child_panel, parent_front, block_map):
    front_full = parent_front.astype(jnp.float32)
    block_tiles = front_full.reshape(PARENT_BLOCKS, BLK, PARENT_BLOCKS, BLK).transpose(0, 2, 1, 3)
    for member in range(CHILDREN):
        factor_rows = child_panel[member]
        contrib = child_update[member] - jnp.dot(factor_rows.astype(jnp.float32), factor_rows.T.astype(jnp.float32), preferred_element_type=jnp.float32)
        pieces = contrib.reshape(CHILD_BLOCKS, BLK, CHILD_BLOCKS, BLK).transpose(0, 2, 1, 3)
        where_to = block_map[member].astype(jnp.int32)
        block_tiles = block_tiles.at[where_to[:, None], where_to[None, :]].add(pieces)
    front_full = block_tiles.transpose(0, 2, 1, 3).reshape(PARENT, PARENT)
    pivot_factor = jnp.linalg.cholesky(front_full[:PANEL, :PANEL])
    solved = jax.scipy.linalg.solve_triangular(pivot_factor, front_full[PANEL:, :PANEL].T, lower=True).T
    panel_full = jnp.concatenate([pivot_factor, solved], axis=0)
    panel_low = panel_full.astype(jnp.bfloat16)
    update_full = front_full - jnp.dot(panel_low.astype(jnp.float32), panel_low.T.astype(jnp.float32), preferred_element_type=jnp.float32)
    indices = jnp.arange(PARENT)
    keep_mask = (indices[:, None] >= PANEL) & (indices[None, :] >= PANEL)
    schur_full = jnp.where(keep_mask, update_full, jnp.zeros_like(update_full))
    return (schur_full, panel_full)
```

```python
import functools
import math

import jax
import jax.numpy as jnp
from jax import lax
from jax.experimental import pallas as pl
from jax.experimental.pallas import tpu as pltpu
from jax.sharding import PartitionSpec as P

BLK = 128
PANEL = 512
PB = PANEL // BLK
PAIR = 2 * BLK
SCALE_ROWS = 16
TOP = 32700.0
STEPS_PER_E = 64.0 / math.log(2.0)
HIGHEST = lax.Precision.HIGHEST
MESH = pl.DeviceIdType.MESH
ANY = pl.BlockSpec(memory_space=pl.ANY)
VMEM = pl.BlockSpec(memory_space=pltpu.VMEM)
SMEM = pl.BlockSpec(memory_space=pltpu.SMEM)


def group_ranks(labels):
    position = jnp.arange(labels.shape[-1])
    before = position[:, None] > position[None, :]
    same_label = labels[..., :, None] == labels[..., None, :]
    return jnp.sum(jnp.logical_and(same_label, before), axis=-1)


def member_of_slot(slot, slots, count):
    hits = (slot[:, None] == jnp.arange(slots)).astype(jnp.int32)
    return jnp.sum(hits * jnp.arange(count, dtype=jnp.int32)[:, None], axis=0)


def slot_of_block(grouped, slot_in_group, cap, first, count):
    groups = grouped.shape[1]
    wanted = first + jnp.arange(count, dtype=jnp.int32)
    hits = grouped[..., None] == wanted
    value = jnp.arange(groups, dtype=jnp.int32)[None, :, None] * cap + slot_in_group
    total = jnp.sum(jnp.where(hits, value[..., None] + 1, 0), axis=(1, 2))
    return total.astype(jnp.int32) - 1


def encode(x):
    peak = jnp.max(jnp.abs(x), axis=0, keepdims=True)
    unit = jnp.ceil(jnp.log(jnp.maximum(peak, 1e-30) * (1.0 / TOP)) * STEPS_PER_E)
    codes = jnp.round(x * jnp.exp(unit * (-1.0 / STEPS_PER_E)))
    return codes.astype(jnp.int32).astype(jnp.int16), unit


def scale_tile(units):
    width = units[0].shape[-1]
    row = lax.broadcasted_iota(jnp.int32, (SCALE_ROWS, width), 0)
    tile = jnp.zeros((SCALE_ROWS, width), jnp.float32)
    for index, unit in enumerate(units):
        tile = jnp.where(row == index, unit, tile)
    return tile.astype(jnp.int32).astype(jnp.int16)


def decode(codes, scales, index):
    scales = scales.astype(jnp.int32).astype(jnp.float32)
    row = lax.broadcasted_iota(jnp.int32, scales.shape, 0)
    unit = jnp.sum(jnp.where(row == index, scales, 0.0), axis=0, keepdims=True)
    return codes.astype(jnp.int32).astype(jnp.float32) * jnp.exp(unit * (1.0 / STEPS_PER_E))


def ring_position(index, count):
    odd = index % 2
    return (1 - odd) * (index // 2) + odd * (count - 1 - index // 2)


def ring_member(position, count):
    position = (position + count) % count
    back = position // (count // 2)
    return (1 - back) * (2 * position) + back * (2 * (count - 1 - position) + 1)


def greet_all(sizes):
    cubes, rows, cols = sizes
    count = cubes * rows * cols
    me = (lax.axis_index("cube") * rows + lax.axis_index("row")) * cols + lax.axis_index("col")
    barrier = pltpu.get_barrier_semaphore()

    def greet(step, carry):
        other = (me + step) % count
        device = (other // (rows * cols), (other // cols) % rows, other % cols)
        pl.semaphore_signal(barrier, inc=1, device_id=device, device_id_type=MESH)
        return carry

    lax.fori_loop(1, count, greet, 0)
    pl.semaphore_wait(barrier, count - 1)
    return me


def send(src, dst, send_sem, recv_sem, device):
    return pltpu.make_async_remote_copy(
        src_ref=src,
        dst_ref=dst,
        send_sem=send_sem,
        recv_sem=recv_sem,
        device_id=device,
        device_id_type=MESH,
    )


def contribute_kernel(
    sizes, tables, own_any, update_any, arrived, own, column, update, product, packed,
    load_sem, pass_send, pass_recv, out_send, out_recv, keep_sem,
):
    cubes, rows, cols, row_cap, col_cap = sizes
    cube, row, col = lax.axis_index("cube"), lax.axis_index("row"), lax.axis_index("col")
    slots = cubes * cols * col_cap
    pairs = slots // 2
    together = min(2, col_cap)
    group_blocks = own.shape[0]
    col_blocks = update.shape[0]
    tile = min(PB, group_blocks)

    def load_update(block):
        left = pl.multiple_of(block * BLK, BLK)
        return pltpu.make_async_copy(
            update_any.at[:, :, pl.ds(left, BLK)], update.at[block], load_sem.at[1 + block]
        )

    load_own = pltpu.make_async_copy(own_any, own, load_sem.at[0])
    load_own.start()

    def start_load(block, carry):
        load_update(block).start()
        return carry

    lax.fori_loop(0, col_blocks, start_load, 0)
    me = greet_all((cubes, rows, cols))
    load_own.wait()

    place = ring_position(row, rows)
    forward_dist = (place - ring_position(col, rows) + rows) % rows
    dists = (forward_dist, (rows - forward_dist) % rows)
    nexts = (ring_member(place + 1, rows), ring_member(place - 1, rows))

    @pl.when(row == col)
    def _():
        def fill(slot, carry):
            column[slot] = own[tables[group_blocks + slot]]
            return carry

        lax.fori_loop(0, slots, fill, 0)

    def pair_at(time):
        rest = (time + pairs - 2 + col) % (pairs - 1) + 1
        first = jnp.where(time == 0, 1, 0)
        return (1 - first) * rest

    def passing(slot, way):
        return send(
            column.at[slot],
            column.at[slot],
            pass_send.at[slot],
            pass_recv.at[slot],
            (cube, nexts[way], col),
        )

    def destination(slot, other_row):
        target = slot // col_cap
        return (target // cols, other_row, target % cols)

    def outgoing(slot, other_row):
        return send(
            packed.at[pl.ds(slot, together), other_row],
            arrived.at[cube, row, col, pl.ds(slot % col_cap, together)],
            out_send.at[slot // together, other_row],
            out_recv.at[me, (slot % col_cap) // together],
            destination(slot, other_row),
        )

    def staying(slot, other_row):
        return pltpu.make_async_copy(
            packed.at[pl.ds(slot, together), other_row],
            arrived.at[cube, row, col, pl.ds(slot % col_cap, together)],
            keep_sem.at[(slot % col_cap) // together],
        )

    def is_mine(slot, other_row):
        to_cube, to_row, to_col = destination(slot, other_row)
        return (to_cube == cube) & (to_row == row) & (to_col == col)

    def work(pair):
        panel = column[pl.ds(2 * pair, 2)].reshape(PAIR, own.shape[2])

        def multiply(step, carry):
            at = pl.ds(step * tile, tile)
            product[at] = lax.dot_general(
                own[at].reshape(tile * BLK, own.shape[2]),
                panel,
                (((1,), (1,)), ((), ())),
                preferred_element_type=jnp.float32,
            ).reshape(tile, BLK, PAIR)
            return carry

        lax.fori_loop(0, group_blocks // tile, multiply, 0)

        def pack(step, carry):
            other_row = (row + 1 + step) % rows
            for half in range(2):
                slot = 2 * pair + half
                left = tables[group_blocks + slot]
                units = []
                for block in range(row_cap):
                    high = tables[other_row * row_cap + block]
                    value = update[left, high] - product[high, :, half * BLK : (half + 1) * BLK]
                    codes, unit = encode(value)
                    packed[slot, other_row, block * BLK : (block + 1) * BLK, :] = codes
                    units.append(unit)
                packed[slot, other_row, row_cap * BLK :, :] = scale_tile(units)
            for part in range(2 // together):
                slot = 2 * pair + part * together
                mine = is_mine(slot, other_row)

                @pl.when(mine)
                def _():
                    staying(slot, other_row).start()

                @pl.when(jnp.logical_not(mine))
                def _():
                    outgoing(slot, other_row).start()

            return carry

        lax.fori_loop(0, rows, pack, 0)

    def turn(time, carry):
        for way in range(2):
            step = time - dists[way]
            ready = (step >= 0) & (step < pairs)
            slot = 2 * pair_at(jnp.clip(step, 0, pairs - 1)) + way

            @pl.when(ready & (dists[way] > 0))
            def _():
                passing(slot, way).wait_recv()

            @pl.when(ready & (dists[way] < rows - 1))
            def _():
                passing(slot, way).start()

        @pl.when(time == rows - 1)
        def _():
            def end_load(block, inner):
                load_update(block).wait()
                return inner

            lax.fori_loop(0, col_blocks, end_load, 0)

        @pl.when(time >= rows - 1)
        def _():
            work(pair_at(jnp.maximum(time - (rows - 1), 0)))

        return carry

    lax.fori_loop(0, pairs + rows - 1, turn, 0)

    for way in range(2):

        @pl.when(dists[way] < rows - 1)
        def _():
            def sent(pair, carry):
                passing(2 * pair + way, way).wait_send()
                return carry

            lax.fori_loop(0, pairs, sent, 0)

    def settle(index, carry):
        slot = (index // rows) * together
        other_row = index % rows
        mine = is_mine(slot, other_row)

        @pl.when(mine)
        def _():
            staying(slot, other_row).wait()

        @pl.when(jnp.logical_not(mine))
        def _():
            outgoing(slot, other_row).wait_send()

        return carry

    lax.fori_loop(0, (slots // together) * rows, settle, 0)

    count = cubes * rows * cols

    def collect(index, carry):
        other = (me + index) % count
        device = (other // (rows * cols), (other // cols) % rows, other % cols)
        for part in range(col_cap // together):
            send(
                packed.at[pl.ds(0, together), 0],
                arrived.at[
                    device[0], device[1], device[2], part * together : (part + 1) * together
                ],
                out_send.at[0, 0],
                out_recv.at[other, part],
                device,
            ).wait_recv()
        return carry

    lax.fori_loop(1, count, collect, 0)


def contribute(own_panel, update, my_rows, my_cols, sizes):
    cubes, rows, cols, row_cap, col_cap = sizes
    slots = cubes * cols * col_cap
    together = min(2, col_cap)
    depth = own_panel.shape[1]
    high, wide = update.shape[0] // BLK, update.shape[1] // BLK
    piece = row_cap * BLK + SCALE_ROWS
    tables = jnp.concatenate([my_rows, my_cols]).astype(jnp.int32)
    return pl.pallas_call(
        functools.partial(contribute_kernel, sizes),
        out_shape=jax.ShapeDtypeStruct((cubes, rows, cols, col_cap, piece, BLK), jnp.int16),
        in_specs=[SMEM, ANY, ANY],
        out_specs=ANY,
        scratch_shapes=[
            pltpu.VMEM((high, BLK, depth), own_panel.dtype),
            pltpu.VMEM((slots, BLK, depth), own_panel.dtype),
            pltpu.VMEM((wide, high, BLK, BLK), jnp.float32),
            pltpu.VMEM((high, BLK, PAIR), jnp.float32),
            pltpu.VMEM((slots, rows, piece, BLK), jnp.int16),
            pltpu.SemaphoreType.DMA((1 + wide,)),
            pltpu.SemaphoreType.DMA((slots,)),
            pltpu.SemaphoreType.DMA((slots,)),
            pltpu.SemaphoreType.DMA((slots // together, rows)),
            pltpu.SemaphoreType.DMA((cubes * rows * cols, col_cap // together)),
            pltpu.SemaphoreType.DMA((col_cap // together,)),
        ],
        compiler_params=pltpu.CompilerParams(
            collective_id=0, has_side_effects=True, vmem_limit_bytes=56 * 2**20
        ),
        name="contribute",
    )(tables, own_panel.reshape(high, BLK, depth), update.reshape(high, BLK, wide * BLK))


def arrivals(layout, tables, arrived, row_block, col_block):
    range_rows, range_cols, row_cap, col_cap = layout
    children = arrived.shape[0]
    found = []
    for child in range(children):
        row_slot = tables[child * range_rows + row_block]
        col_slot = tables[children * range_rows + child * range_cols + col_block]
        row_at, col_at = jnp.maximum(row_slot, 0), jnp.maximum(col_slot, 0)
        place = (child, row_at // row_cap, col_at // col_cap, col_at % col_cap)
        block = row_at % row_cap

        def piece(place=place, block=block):
            codes = arrived[place + (pl.ds(pl.multiple_of(block * BLK, BLK), BLK), slice(None))]
            scales = arrived[place + (pl.ds(row_cap * BLK, SCALE_ROWS), slice(None))]
            return decode(codes, scales, block)

        found.append(((row_slot >= 0) & (col_slot >= 0), piece))
    return found


def assemble_kernel(
    layout, tables, arrived, parent_any, strip_out, top_out, pivot_out, strip, top, total, sems
):
    range_rows, range_cols = layout[:2]
    loads = (
        pltpu.make_async_copy(parent_any.at[:, pl.ds(0, PANEL)], strip, sems.at[0]),
        pltpu.make_async_copy(parent_any.at[pl.ds(0, PANEL), :], top, sems.at[1]),
    )
    for load in loads:
        load.start()

    def gather(row_block, col_block, parent, at):
        total[:, at] = parent.astype(jnp.float32)
        for valid, piece in arrivals(layout, tables, arrived, row_block, col_block):

            @pl.when(valid)
            def _(piece=piece):
                total[:, at] += piece()

    loads[0].wait()

    def strip_rows(step, carry):
        for half in range(2):
            row_block = 2 * step + half
            high = pl.multiple_of(row_block * BLK, BLK)
            units = []
            for block in range(PB):
                at = slice(block * BLK, (block + 1) * BLK)
                gather(row_block, block, strip[pl.ds(high, BLK), at], at)
            codes, unit = encode(total[:, :PANEL])
            strip_out[step, half * BLK : (half + 1) * BLK, :] = codes
            row = lax.broadcasted_iota(jnp.int32, (SCALE_ROWS, PANEL), 0)
            strip_units = jnp.where(row == half, unit, 0.0 if half == 0 else strip_units)

            for block in range(PB):

                @pl.when(row_block == block)
                def _():
                    for other in range(block, PB):
                        pivot_out[block * PB + other] = total[:, other * BLK : (other + 1) * BLK]

        strip_out[step, PAIR:, :] = strip_units.astype(jnp.int32).astype(jnp.int16)
        return carry

    lax.fori_loop(0, range_rows // 2, strip_rows, 0)
    loads[1].wait()

    def top_cols(step, carry):
        units = []
        for block in range(PB):
            for half in range(2):
                col_block = 2 * step + half
                left = pl.multiple_of(col_block * BLK, BLK)
                at = slice(half * BLK, (half + 1) * BLK)
                gather(
                    block, col_block, top[block * BLK : (block + 1) * BLK, pl.ds(left, BLK)], at
                )
            codes, unit = encode(total[:, :PAIR])
            top_out[step, block * BLK : (block + 1) * BLK, :] = codes
            units.append(unit)
        top_out[step, PANEL:, :] = scale_tile(units)
        return carry

    lax.fori_loop(0, range_cols // 2, top_cols, 0)


def assemble(tables, arrived, parent, layout):
    range_rows, range_cols = layout[:2]
    return pl.pallas_call(
        functools.partial(assemble_kernel, layout),
        out_shape=(
            jax.ShapeDtypeStruct((range_rows // 2, PAIR + SCALE_ROWS, PANEL), jnp.int16),
            jax.ShapeDtypeStruct((range_cols // 2, PANEL + SCALE_ROWS, PAIR), jnp.int16),
            jax.ShapeDtypeStruct((PB * PB, BLK, BLK), jnp.float32),
        ),
        in_specs=[SMEM, VMEM, ANY],
        out_specs=(VMEM, VMEM, VMEM),
        scratch_shapes=[
            pltpu.VMEM((range_rows * BLK, PANEL), parent.dtype),
            pltpu.VMEM((PANEL, range_cols * BLK), parent.dtype),
            pltpu.VMEM((BLK, PANEL), jnp.float32),
            pltpu.SemaphoreType.DMA((2,)),
        ],
        compiler_params=pltpu.CompilerParams(vmem_limit_bytes=50 * 2**20),
        name="assemble",
    )(tables, arrived, parent)


SUB = 8
SUBS = BLK // SUB


def eliminate_rows(step, diagonal):
    at = pl.ds(pl.multiple_of(step * SUB, SUB), SUB)
    rows = diagonal[at, :]
    small = pltpu.roll(rows[:, :BLK], (BLK - step * SUB) % BLK, 1)
    sub = lax.broadcasted_iota(jnp.int32, (SUB, 1), 0)
    for index in range(SUB):
        pivot = small[index : index + 1, index : index + 1]
        root = lax.rsqrt(pivot)
        root = root * (1.5 - 0.5 * pivot * root * root)
        scaled = rows[index : index + 1, :] * root
        scaled_small = small[index : index + 1, :] * root
        factor = jnp.where(sub > index, small[:, index : index + 1] * root, 0.0)
        rows = jnp.where(sub == index, scaled, rows - factor * scaled)
        small = jnp.where(sub == index, scaled_small, small - factor * scaled_small)
    diagonal[at, :] = rows
    lane = lax.broadcasted_iota(jnp.int32, (SUB, BLK), 1)
    left = jnp.where(lane >= (step + 1) * SUB, rows[:, :BLK], 0.0)
    diagonal[...] -= lax.dot_general(
        left, rows, (((0,), (0,)), ((), ())), precision=HIGHEST, preferred_element_type=jnp.float32
    )


def finish_block(block, whole, diagonal):
    at = pl.ds(pl.multiple_of(block * BLK, BLK), BLK)
    solved = jnp.dot(
        diagonal[:, BLK:], whole[at, :], precision=HIGHEST, preferred_element_type=jnp.float32
    )
    whole[at, :] = solved
    for below in range(1, PB):

        @pl.when(below > block)
        def _():
            whole[below * BLK : (below + 1) * BLK, :] -= lax.dot_general(
                whole[at, below * BLK : (below + 1) * BLK],
                whole[at, :],
                (((0,), (0,)), ((), ())),
                precision=HIGHEST,
                preferred_element_type=jnp.float32,
            )


def start_block(block, whole, diagonal):
    at = pl.ds(pl.multiple_of(block * BLK, BLK), BLK)
    diagonal[:, :BLK] = whole[at, at]
    eye = lax.broadcasted_iota(jnp.int32, (BLK, BLK), 0) == lax.broadcasted_iota(
        jnp.int32, (BLK, BLK), 1
    )
    diagonal[:, BLK:] = eye.astype(jnp.float32)


def factor_kernel(
    sizes, strip_in, top_any, pivot_any, strip_all, lower_out, inverse_out, low_out,
    top, pivot, whole, diagonal, load_sem, pivot_send, pivot_recv, top_send, top_recv,
    strip_send, strip_recv,
):
    cubes, rows, cols = sizes
    cube, row, col = lax.axis_index("cube"), lax.axis_index("row"), lax.axis_index("col")
    strips, tops = strip_all.shape[0], top.shape[0]
    upper = [i * PB + j for i in range(PB) for j in range(i, PB)]
    root = (cube == 0) & (row == 0) & (col == 0)

    @pl.when(root)
    def _():
        load = pltpu.make_async_copy(pivot_any, pivot, load_sem.at[0])
        load.start()
        load.wait()

    @pl.when(row == 0)
    def _():
        load = pltpu.make_async_copy(top_any, top, load_sem.at[1])
        load.start()
        load.wait()

    greet_all(sizes)

    place = ring_position(row, rows)
    half = rows // 2
    ahead, behind = ring_member(place + 1, rows), ring_member(place - 1, rows)
    back = (place + rows - 1) % rows
    children = [
        ((cube == 0) & (row == 0) & (col < cols - 1), (0, 0, col + 1)),
        ((cube == 0) & (place < half), (0, ahead, col)),
        ((cube == 0) & ((place == 0) | (place > half)) & (back > half), (0, behind, col)),
    ] + [(cube == 0, (other, row, col)) for other in range(1, cubes)]

    def pivot_copy(block, child):
        return send(
            pivot.at[block],
            pivot.at[block],
            pivot_send.at[block, child],
            pivot_recv.at[block],
            children[child][1],
        )

    for block in upper:

        @pl.when(jnp.logical_not(root))
        def _():
            pivot_copy(block, 0).wait_recv()

        for child, (active, _) in enumerate(children):

            @pl.when(active)
            def _():
                pivot_copy(block, child).start()

    whole[...] = jnp.zeros_like(whole)
    for i in range(PB):
        for j in range(i, PB):
            whole[i * BLK : (i + 1) * BLK, j * BLK : (j + 1) * BLK] = pivot[i * PB + j]
        eye = lax.broadcasted_iota(jnp.int32, (BLK, BLK), 0) == lax.broadcasted_iota(
            jnp.int32, (BLK, BLK), 1
        )
        whole[i * BLK : (i + 1) * BLK, PANEL + i * BLK : PANEL + (i + 1) * BLK] = eye.astype(
            jnp.float32
        )

    dists = (place, (rows - place) % rows)
    nexts = (ahead, behind)

    def top_copy(index, way):
        return send(
            top.at[index], top.at[index], top_send.at[index], top_recv.at[index],
            (cube, nexts[way], col),
        )

    strip_active = [(cube == 0) & (col < cols - 1)] + [cube == 0] * (cubes - 1)
    strip_got = (cube > 0) | (col > 0)

    def strip_copy(index, child):
        device = (0, row, col + 1) if child == 0 else (child, row, col)
        return send(
            strip_all.at[index], strip_all.at[index], strip_send.at[index, child],
            strip_recv.at[index], device,
        )

    turns = max(strips + cols, 2 * (tops // 2 + rows - 1))
    each = -(-PB * SUBS // turns)

    def turn(time, carry):
        index = time - col - jnp.where(cube > 0, 1, 0)
        ready = (index >= 0) & (index < strips)
        index = jnp.clip(index, 0, strips - 1)

        @pl.when(ready & strip_got)
        def _():
            strip_copy(index, 0).wait_recv()

        for child, active in enumerate(strip_active):

            @pl.when(ready & active)
            def _():
                strip_copy(index, child).start()

        for way in range(2):
            step = time // 2 - dists[way]
            due = (time % 2 == 0) & (step >= 0) & (step < tops // 2)
            chunk = 2 * jnp.clip(step, 0, tops // 2 - 1) + way

            @pl.when(due & (dists[way] > 0))
            def _():
                top_copy(chunk, way).wait_recv()

            @pl.when(due & (dists[way] < rows - 1))
            def _():
                top_copy(chunk, way).start()

        def advance(sub, inner):
            step = time * each + sub
            block = step // SUBS

            @pl.when(step < PB * SUBS)
            def _():
                @pl.when(step % SUBS == 0)
                def _():
                    start_block(block, whole, diagonal)

                eliminate_rows(step % SUBS, diagonal)

                @pl.when(step % SUBS == SUBS - 1)
                def _():
                    finish_block(block, whole, diagonal)

            return inner

        lax.fori_loop(0, each, advance, 0)
        return carry

    lax.fori_loop(0, turns, turn, 0)

    inverse_out[...] = whole[:, PANEL:]
    lower_out[...] = jnp.zeros_like(lower_out)
    for i in range(PB):
        for j in range(i + 1):
            block = whole[j * BLK : (j + 1) * BLK, i * BLK : (i + 1) * BLK].T
            if i == j:
                keep = lax.broadcasted_iota(jnp.int32, (BLK, BLK), 0) >= lax.broadcasted_iota(
                    jnp.int32, (BLK, BLK), 1
                )
                block = jnp.where(keep, block, 0.0)
            lower_out[i * BLK : (i + 1) * BLK, j * BLK : (j + 1) * BLK] = block

    def solve(index, carry):
        parts = [
            decode(top[index, b * BLK : (b + 1) * BLK, :], top[index, PANEL:, :], b)
            for b in range(PB)
        ]
        solved = jnp.dot(
            inverse_out[...],
            jnp.concatenate(parts, axis=0),
            precision=HIGHEST,
            preferred_element_type=jnp.float32,
        )
        low_out[:, pl.ds(pl.multiple_of(index * PAIR, PAIR), PAIR)] = solved.astype(low_out.dtype)
        return carry

    lax.fori_loop(0, tops, solve, 0)

    for block in upper:
        for child, (active, _) in enumerate(children):

            @pl.when(active)
            def _():
                pivot_copy(block, child).wait_send()

    def strips_sent(index, carry):
        for child, active in enumerate(strip_active):

            @pl.when(active)
            def _():
                strip_copy(index, child).wait_send()

        return carry

    lax.fori_loop(0, strips, strips_sent, 0)
    for way in range(2):

        @pl.when(dists[way] < rows - 1)
        def _():
            def tops_sent(index, carry):
                top_copy(2 * index + way, way).wait_send()
                return carry

            lax.fori_loop(0, tops // 2, tops_sent, 0)


def factor(strip, top, pivot, sizes):
    cubes = sizes[0]
    square = jax.ShapeDtypeStruct((PANEL, PANEL), jnp.float32)
    return pl.pallas_call(
        functools.partial(factor_kernel, sizes),
        out_shape=(
            jax.ShapeDtypeStruct(strip.shape, strip.dtype),
            square,
            square,
            jax.ShapeDtypeStruct((PANEL, top.shape[0] * PAIR), jnp.bfloat16),
        ),
        in_specs=[ANY, ANY, ANY],
        out_specs=(ANY, VMEM, VMEM, VMEM),
        input_output_aliases={0: 0},
        scratch_shapes=[
            pltpu.VMEM(top.shape, top.dtype),
            pltpu.VMEM(pivot.shape, pivot.dtype),
            pltpu.VMEM((PANEL, 2 * PANEL), jnp.float32),
            pltpu.VMEM((BLK, 2 * BLK), jnp.float32),
            pltpu.SemaphoreType.DMA((2,)),
            pltpu.SemaphoreType.DMA((PB * PB, 2 + cubes)),
            pltpu.SemaphoreType.DMA((PB * PB,)),
            pltpu.SemaphoreType.DMA((top.shape[0],)),
            pltpu.SemaphoreType.DMA((top.shape[0],)),
            pltpu.SemaphoreType.DMA((strip.shape[0], cubes)),
            pltpu.SemaphoreType.DMA((strip.shape[0],)),
        ],
        compiler_params=pltpu.CompilerParams(
            collective_id=1, has_side_effects=True, vmem_limit_bytes=50 * 2**20
        ),
        name="factor",
    )(strip, top, pivot)


def final_kernel(
    layout, tables, parent, strip, lower, inverse, low, arrived, schur, panel, solved
):
    range_rows, range_cols = layout[:2]
    step = pl.program_id(0)
    base = arrived.shape[0] * (range_rows + range_cols)
    first_row, first_col = tables[base], tables[base + 1]
    right = jnp.concatenate(
        [decode(strip[0, b * BLK : (b + 1) * BLK, :], strip[0, PAIR:, :], b) for b in range(2)],
        axis=0,
    )
    solved[...] = lax.dot_general(
        right,
        inverse[...],
        (((1,), (1,)), ((), ())),
        precision=HIGHEST,
        preferred_element_type=jnp.float32,
    )

    @pl.when(first_row + 2 * step < PB)
    def _():
        solved[...] = lower[...]

    panel[...] = solved[...]
    schur[...] = jnp.dot(
        solved[...].astype(jnp.bfloat16), low[...], preferred_element_type=jnp.float32
    )
    for half in range(2):
        row_block = 2 * step + half
        high = slice(half * BLK, (half + 1) * BLK)
        for block in range(range_cols):
            at = slice(block * BLK, (block + 1) * BLK)
            keep = (first_row + row_block >= PB) & (first_col + block >= PB)
            left = parent[high, at].astype(jnp.float32) - schur[high, at]
            schur[high, at] = jnp.where(keep, left, 0.0)
            for valid, piece in arrivals(layout, tables, arrived, row_block, block):

                @pl.when(valid & keep)
                def _(piece=piece):
                    schur[high, at] += piece()


def final(tables, parent, strip, lower, inverse, low, arrived, layout):
    height, width = parent.shape
    return pl.pallas_call(
        functools.partial(final_kernel, layout),
        out_shape=(
            jax.ShapeDtypeStruct((height, width), jnp.float32),
            jax.ShapeDtypeStruct((height, PANEL), jnp.float32),
        ),
        grid_spec=pltpu.PrefetchScalarGridSpec(
            num_scalar_prefetch=1,
            grid=(height // PAIR,),
            in_specs=[
                pl.BlockSpec((PAIR, width), lambda s, t: (s, 0)),
                pl.BlockSpec((1,) + strip.shape[1:], lambda s, t: (s, 0, 0)),
                pl.BlockSpec((PAIR, PANEL), lambda s, t: (jnp.minimum(s, PANEL // PAIR - 1), 0)),
                VMEM,
                VMEM,
                VMEM,
            ],
            out_specs=(
                pl.BlockSpec((PAIR, width), lambda s, t: (s, 0)),
                pl.BlockSpec((PAIR, PANEL), lambda s, t: (s, 0)),
            ),
            scratch_shapes=[pltpu.VMEM((PAIR, PANEL), jnp.float32)],
        ),
        compiler_params=pltpu.CompilerParams(vmem_limit_bytes=50 * 2**20),
        name="final",
    )(tables, parent, strip, lower, inverse, low, arrived)


def body(child_update, child_panel, parent_front, block_map):
    rows = lax.axis_size("row")
    cubes = lax.axis_size("cube")
    cols = lax.axis_size("col")
    ranges = cubes * cols
    child_index = lax.axis_index("cube")
    row_index = lax.axis_index("row")
    col_index = lax.axis_index("col")
    range_index = lax.axis_index(("cube", "col"))
    group_blocks = child_update.shape[1] // BLK
    row_cap = group_blocks // rows
    col_cap = max(1, group_blocks // ranges)
    range_rows = parent_front.shape[0] // BLK
    range_cols = parent_front.shape[1] // BLK

    children = block_map.shape[0]
    grouped = block_map.reshape(children, rows, group_blocks)
    row_dest = grouped // range_rows
    col_dest = grouped // range_cols
    row_slot = row_dest * row_cap + group_ranks(row_dest)
    col_rank = group_ranks(col_dest)
    row_rank = row_slot - row_dest * row_cap
    col_slot = col_dest * col_cap + col_rank
    my_rows = member_of_slot(row_slot[child_index, row_index], group_blocks, group_blocks)
    my_cols = member_of_slot(col_slot[child_index, col_index], ranges * col_cap, group_blocks)
    from_rows = slot_of_block(grouped, row_rank, row_cap, row_index * range_rows, range_rows)
    from_cols = slot_of_block(grouped, col_rank, col_cap, range_index * range_cols, range_cols)
    tables = jnp.concatenate(
        [
            from_rows.reshape(-1),
            from_cols.reshape(-1),
            jnp.stack([row_index * range_rows, range_index * range_cols]),
        ]
    ).astype(jnp.int32)

    arrived = contribute(
        child_panel[0], child_update[0], my_rows, my_cols, (cubes, rows, cols, row_cap, col_cap)
    )
    layout = (range_rows, range_cols, row_cap, col_cap)
    strip, top, pivot = assemble(tables, arrived, parent_front, layout)
    strip, lower, inverse, low = factor(strip, top, pivot, (cubes, rows, cols))
    return final(tables, parent_front, strip, lower, inverse, low, arrived, layout)


def solution(mesh):
    placed = (P("cube", "row", "col"), P("cube", "row", None), P("row", ("cube", "col")), P())
    return jax.shard_map(
        body,
        mesh=mesh,
        in_specs=placed,
        out_specs=(P("row", ("cube", "col")), P("row", None)),
        check_vma=False,
    )
```

```python
import functools
import math

import jax
import jax.numpy as jnp
from jax import lax
from jax.experimental import pallas as pl
from jax.experimental.pallas import tpu as pltpu
from jax.sharding import PartitionSpec as P

BLK = 128
PANEL = 512
PB = PANEL // BLK
PAIR = 2 * BLK
SCALE_ROWS = 16
TOP = 32700.0
STEPS_PER_E = 64.0 / math.log(2.0)
HIGHEST = lax.Precision.HIGHEST
MESH = pl.DeviceIdType.MESH
ANY = pl.BlockSpec(memory_space=pl.ANY)
VMEM = pl.BlockSpec(memory_space=pltpu.VMEM)
SMEM = pl.BlockSpec(memory_space=pltpu.SMEM)


def group_ranks(labels):
    position = jnp.arange(labels.shape[-1])
    before = position[:, None] > position[None, :]
    same_label = labels[..., :, None] == labels[..., None, :]
    return jnp.sum(jnp.logical_and(same_label, before), axis=-1)


def member_of_slot(slot, slots, count):
    hits = (slot[:, None] == jnp.arange(slots)).astype(jnp.int32)
    return jnp.sum(hits * jnp.arange(count, dtype=jnp.int32)[:, None], axis=0)


def slot_of_block(grouped, slot_in_group, cap, first, count):
    groups = grouped.shape[1]
    wanted = first + jnp.arange(count, dtype=jnp.int32)
    hits = grouped[..., None] == wanted
    value = jnp.arange(groups, dtype=jnp.int32)[None, :, None] * cap + slot_in_group
    total = jnp.sum(jnp.where(hits, value[..., None] + 1, 0), axis=(1, 2))
    return total.astype(jnp.int32) - 1


def encode(x):
    peak = jnp.max(jnp.abs(x), axis=0, keepdims=True)
    unit = jnp.ceil(jnp.log(jnp.maximum(peak, 1e-30) * (1.0 / TOP)) * STEPS_PER_E)
    codes = jnp.round(x * jnp.exp(unit * (-1.0 / STEPS_PER_E)))
    return codes.astype(jnp.int32).astype(jnp.int16), unit


def scale_tile(units):
    width = units[0].shape[-1]
    row = lax.broadcasted_iota(jnp.int32, (SCALE_ROWS, width), 0)
    tile = jnp.zeros((SCALE_ROWS, width), jnp.float32)
    for index, unit in enumerate(units):
        tile = jnp.where(row == index, unit, tile)
    return tile.astype(jnp.int32).astype(jnp.int16)


def decode(codes, scales, index):
    scales = scales.astype(jnp.int32).astype(jnp.float32)
    row = lax.broadcasted_iota(jnp.int32, scales.shape, 0)
    unit = jnp.sum(jnp.where(row == index, scales, 0.0), axis=0, keepdims=True)
    return codes.astype(jnp.int32).astype(jnp.float32) * jnp.exp(unit * (1.0 / STEPS_PER_E))


def ring_position(index, count):
    odd = index % 2
    return (1 - odd) * (index // 2) + odd * (count - 1 - index // 2)


def ring_member(position, count):
    position = (position + count) % count
    back = position // (count // 2)
    return (1 - back) * (2 * position) + back * (2 * (count - 1 - position) + 1)


def greet_all(sizes):
    cubes, rows, cols = sizes
    count = cubes * rows * cols
    me = (lax.axis_index("cube") * rows + lax.axis_index("row")) * cols + lax.axis_index("col")
    barrier = pltpu.get_barrier_semaphore()

    def greet(step, carry):
        other = (me + step) % count
        device = (other // (rows * cols), (other // cols) % rows, other % cols)
        pl.semaphore_signal(barrier, inc=1, device_id=device, device_id_type=MESH)
        return carry

    lax.fori_loop(1, count, greet, 0)
    pl.semaphore_wait(barrier, count - 1)
    return me


def send(src, dst, send_sem, recv_sem, device):
    return pltpu.make_async_remote_copy(
        src_ref=src,
        dst_ref=dst,
        send_sem=send_sem,
        recv_sem=recv_sem,
        device_id=device,
        device_id_type=MESH,
    )


def pair_at(time, pairs, col):
    return ((pairs - 1) * time + col + 3) % pairs


def contribute_kernel(
    sizes, tables, own_any, update_any, arrived, own, column, update, product, packed,
    load_sem, pass_send, pass_recv, out_send, out_recv, keep_sem,
):
    cubes, rows, cols, row_cap, col_cap = sizes
    cube, row, col = lax.axis_index("cube"), lax.axis_index("row"), lax.axis_index("col")
    slots = cubes * cols * col_cap
    pairs = slots // 2
    together = min(2, col_cap)
    group_blocks = own.shape[0]
    col_blocks = update.shape[0]
    tile = min(PB, group_blocks)

    def load_update(block):
        left = pl.multiple_of(block * BLK, BLK)
        return pltpu.make_async_copy(
            update_any.at[:, :, pl.ds(left, BLK)], update.at[block], load_sem.at[1 + block]
        )

    load_own = pltpu.make_async_copy(own_any, own, load_sem.at[0])
    load_own.start()

    def start_load(block, carry):
        load_update(block).start()
        return carry

    lax.fori_loop(0, col_blocks, start_load, 0)
    me = greet_all((cubes, rows, cols))
    load_own.wait()

    place = ring_position(row, rows)
    forward_dist = (place - ring_position(col, rows) + rows) % rows
    dists = (forward_dist, (rows - forward_dist) % rows)
    nexts = (ring_member(place + 1, rows), ring_member(place - 1, rows))

    @pl.when(row == col)
    def _():
        def fill(slot, carry):
            column[slot] = own[tables[group_blocks + slot]]
            return carry

        lax.fori_loop(0, slots, fill, 0)

    def passing(slot, way):
        return send(
            column.at[slot],
            column.at[slot],
            pass_send.at[slot],
            pass_recv.at[slot],
            (cube, nexts[way], col),
        )

    def destination(slot, other_row):
        target = slot // col_cap
        return (target // cols, other_row, target % cols)

    def outgoing(slot, other_row):
        return send(
            packed.at[pl.ds(slot, together), other_row],
            arrived.at[cube, row, col, pl.ds(slot % col_cap, together)],
            out_send.at[slot // together, other_row],
            out_recv.at[me, (slot % col_cap) // together],
            destination(slot, other_row),
        )

    def staying(slot, other_row):
        return pltpu.make_async_copy(
            packed.at[pl.ds(slot, together), other_row],
            arrived.at[cube, row, col, pl.ds(slot % col_cap, together)],
            keep_sem.at[(slot % col_cap) // together],
        )

    def is_mine(slot, other_row):
        to_cube, to_row, to_col = destination(slot, other_row)
        return (to_cube == cube) & (to_row == row) & (to_col == col)

    def work(time):
        pair = pair_at(time, pairs, col)
        panel = column[pl.ds(2 * pair, 2)].reshape(PAIR, own.shape[2])

        def multiply(step, carry):
            at = pl.ds(step * tile, tile)
            product[at] = lax.dot_general(
                own[at].reshape(tile * BLK, own.shape[2]),
                panel,
                (((1,), (1,)), ((), ())),
                preferred_element_type=jnp.float32,
            ).reshape(tile, BLK, PAIR)
            return carry

        lax.fori_loop(0, group_blocks // tile, multiply, 0)

        def pack(step, carry):
            other_row = (row + 1 + step) % rows
            for half in range(2):
                slot = 2 * pair + half
                left = tables[group_blocks + slot]
                units = []
                for block in range(row_cap):
                    high = tables[other_row * row_cap + block]
                    value = update[left, high] - product[high, :, half * BLK : (half + 1) * BLK]
                    codes, unit = encode(value)
                    packed[slot, other_row, block * BLK : (block + 1) * BLK, :] = codes
                    units.append(unit)
                packed[slot, other_row, row_cap * BLK :, :] = scale_tile(units)
            for part in range(2 // together):
                slot = 2 * pair + part * together
                mine = is_mine(slot, other_row)

                @pl.when(mine)
                def _():
                    staying(slot, other_row).start()

                @pl.when(jnp.logical_not(mine))
                def _():
                    outgoing(slot, other_row).start()

            return carry

        lax.fori_loop(0, rows, pack, 0)

    def turn(time, carry):
        for way in range(2):
            step = time - dists[way]
            ready = (step >= 0) & (step < pairs)
            slot = 2 * pair_at(jnp.clip(step, 0, pairs - 1), pairs, col) + way

            @pl.when(ready & (dists[way] > 0))
            def _():
                passing(slot, way).wait_recv()

            @pl.when(ready & (dists[way] < rows - 1))
            def _():
                passing(slot, way).start()

        @pl.when(time == rows - 1)
        def _():
            def end_load(block, inner):
                load_update(block).wait()
                return inner

            lax.fori_loop(0, col_blocks, end_load, 0)

        @pl.when(time >= rows - 1)
        def _():
            work(jnp.maximum(time - (rows - 1), 0))

        return carry

    lax.fori_loop(0, pairs + rows - 1, turn, 0)

    for way in range(2):

        @pl.when(dists[way] < rows - 1)
        def _():
            def sent(pair, carry):
                passing(2 * pair + way, way).wait_send()
                return carry

            lax.fori_loop(0, pairs, sent, 0)

    def settle(index, carry):
        slot = (index // rows) * together
        other_row = index % rows
        mine = is_mine(slot, other_row)

        @pl.when(mine)
        def _():
            staying(slot, other_row).wait()

        @pl.when(jnp.logical_not(mine))
        def _():
            outgoing(slot, other_row).wait_send()

        return carry

    lax.fori_loop(0, (slots // together) * rows, settle, 0)

    count = cubes * rows * cols

    def collect(index, carry):
        other = (me + index) % count
        device = (other // (rows * cols), (other // cols) % rows, other % cols)
        for part in range(col_cap // together):
            send(
                packed.at[pl.ds(0, together), 0],
                arrived.at[
                    device[0], device[1], device[2], part * together : (part + 1) * together
                ],
                out_send.at[0, 0],
                out_recv.at[other, part],
                device,
            ).wait_recv()
        return carry

    lax.fori_loop(1, count, collect, 0)


def contribute(own_panel, update, my_rows, my_cols, sizes):
    cubes, rows, cols, row_cap, col_cap = sizes
    slots = cubes * cols * col_cap
    together = min(2, col_cap)
    depth = own_panel.shape[1]
    high, wide = update.shape[0] // BLK, update.shape[1] // BLK
    piece = row_cap * BLK + SCALE_ROWS
    tables = jnp.concatenate([my_rows, my_cols]).astype(jnp.int32)
    return pl.pallas_call(
        functools.partial(contribute_kernel, sizes),
        out_shape=jax.ShapeDtypeStruct((cubes, rows, cols, col_cap, piece, BLK), jnp.int16),
        in_specs=[SMEM, ANY, ANY],
        out_specs=ANY,
        scratch_shapes=[
            pltpu.VMEM((high, BLK, depth), own_panel.dtype),
            pltpu.VMEM((slots, BLK, depth), own_panel.dtype),
            pltpu.VMEM((wide, high, BLK, BLK), jnp.float32),
            pltpu.VMEM((high, BLK, PAIR), jnp.float32),
            pltpu.VMEM((slots, rows, piece, BLK), jnp.int16),
            pltpu.SemaphoreType.DMA((1 + wide,)),
            pltpu.SemaphoreType.DMA((slots,)),
            pltpu.SemaphoreType.DMA((slots,)),
            pltpu.SemaphoreType.DMA((slots // together, rows)),
            pltpu.SemaphoreType.DMA((cubes * rows * cols, col_cap // together)),
            pltpu.SemaphoreType.DMA((col_cap // together,)),
        ],
        compiler_params=pltpu.CompilerParams(
            collective_id=0, has_side_effects=True, vmem_limit_bytes=56 * 2**20
        ),
        name="contribute",
    )(tables, own_panel.reshape(high, BLK, depth), update.reshape(high, BLK, wide * BLK))


def arrivals(layout, tables, arrived, row_block, col_block):
    range_rows, range_cols, row_cap, col_cap = layout
    children = arrived.shape[0]
    found = []
    for child in range(children):
        row_slot = tables[child * range_rows + row_block]
        col_slot = tables[children * range_rows + child * range_cols + col_block]
        row_at, col_at = jnp.maximum(row_slot, 0), jnp.maximum(col_slot, 0)
        place = (child, row_at // row_cap, col_at // col_cap, col_at % col_cap)
        block = row_at % row_cap

        def piece(place=place, block=block):
            codes = arrived[place + (pl.ds(pl.multiple_of(block * BLK, BLK), BLK), slice(None))]
            scales = arrived[place + (pl.ds(row_cap * BLK, SCALE_ROWS), slice(None))]
            return decode(codes, scales, block)

        found.append(((row_slot >= 0) & (col_slot >= 0), piece))
    return found


def assemble_kernel(layout, tables, arrived, parent_any, strip_out, pivot_out, strip, total, sem):
    range_rows = layout[0]
    load = pltpu.make_async_copy(parent_any.at[:, pl.ds(0, PANEL)], strip, sem.at[0])
    load.start()
    load.wait()

    def strip_rows(step, carry):
        tile = jnp.zeros((SCALE_ROWS, PANEL), jnp.float32)
        for half in range(2):
            row_block = 2 * step + half
            high = pl.multiple_of(row_block * BLK, BLK)
            total[...] = strip[pl.ds(high, BLK), :].astype(jnp.float32)
            for block in range(PB):
                at = slice(block * BLK, (block + 1) * BLK)
                for valid, piece in arrivals(layout, tables, arrived, row_block, block):

                    @pl.when(valid)
                    def _(piece=piece):
                        total[:, at] += piece()

            codes, unit = encode(total[...])
            strip_out[step, half * BLK : (half + 1) * BLK, :] = codes
            row = lax.broadcasted_iota(jnp.int32, (SCALE_ROWS, PANEL), 0)
            tile = jnp.where(row == half, unit, tile)
            for block in range(PB):

                @pl.when(row_block == block)
                def _():
                    for other in range(block, PB):
                        pivot_out[block * PB + other] = total[:, other * BLK : (other + 1) * BLK]

        strip_out[step, PAIR:, :] = tile.astype(jnp.int32).astype(jnp.int16)
        return carry

    lax.fori_loop(0, range_rows // 2, strip_rows, 0)


def assemble(tables, arrived, parent, layout):
    range_rows = layout[0]
    return pl.pallas_call(
        functools.partial(assemble_kernel, layout),
        out_shape=(
            jax.ShapeDtypeStruct((range_rows // 2, PAIR + SCALE_ROWS, PANEL), jnp.int16),
            jax.ShapeDtypeStruct((PB * PB, BLK, BLK), jnp.float32),
        ),
        in_specs=[SMEM, VMEM, ANY],
        out_specs=(VMEM, VMEM),
        scratch_shapes=[
            pltpu.VMEM((range_rows * BLK, PANEL), parent.dtype),
            pltpu.VMEM((BLK, PANEL), jnp.float32),
            pltpu.SemaphoreType.DMA((1,)),
        ],
        compiler_params=pltpu.CompilerParams(vmem_limit_bytes=50 * 2**20),
        name="assemble",
    )(tables, arrived, parent)


SUB = 8
SUBS = BLK // SUB


def eliminate_rows(step, diagonal):
    at = pl.ds(pl.multiple_of(step * SUB, SUB), SUB)
    rows = diagonal[at, :]
    small = pltpu.roll(rows[:, :BLK], (BLK - step * SUB) % BLK, 1)
    sub = lax.broadcasted_iota(jnp.int32, (SUB, 1), 0)
    for index in range(SUB):
        pivot = small[index : index + 1, index : index + 1]
        root = lax.rsqrt(pivot)
        root = root * (1.5 - 0.5 * pivot * root * root)
        scaled = rows[index : index + 1, :] * root
        scaled_small = small[index : index + 1, :] * root
        factor = jnp.where(sub > index, small[:, index : index + 1] * root, 0.0)
        rows = jnp.where(sub == index, scaled, rows - factor * scaled)
        small = jnp.where(sub == index, scaled_small, small - factor * scaled_small)
    diagonal[at, :] = rows
    lane = lax.broadcasted_iota(jnp.int32, (SUB, BLK), 1)
    left = jnp.where(lane >= (step + 1) * SUB, rows[:, :BLK], 0.0)
    diagonal[...] -= lax.dot_general(
        left, rows, (((0,), (0,)), ((), ())), precision=HIGHEST, preferred_element_type=jnp.float32
    )


def finish_block(block, whole, diagonal):
    at = pl.ds(pl.multiple_of(block * BLK, BLK), BLK)
    solved = jnp.dot(
        diagonal[:, BLK:], whole[at, :], precision=HIGHEST, preferred_element_type=jnp.float32
    )
    whole[at, :] = solved
    for below in range(1, PB):

        @pl.when(below > block)
        def _():
            whole[below * BLK : (below + 1) * BLK, :] -= lax.dot_general(
                whole[at, below * BLK : (below + 1) * BLK],
                whole[at, :],
                (((0,), (0,)), ((), ())),
                precision=HIGHEST,
                preferred_element_type=jnp.float32,
            )


def start_block(block, whole, diagonal):
    at = pl.ds(pl.multiple_of(block * BLK, BLK), BLK)
    diagonal[:, :BLK] = whole[at, at]
    eye = lax.broadcasted_iota(jnp.int32, (BLK, BLK), 0) == lax.broadcasted_iota(
        jnp.int32, (BLK, BLK), 1
    )
    diagonal[:, BLK:] = eye.astype(jnp.float32)


def split(x):
    high = x.astype(jnp.bfloat16)
    return high, (x - high.astype(jnp.float32)).astype(jnp.bfloat16)


def times_transposed(x, high, low):
    x_high, x_low = split(x)

    def product(a, b):
        return lax.dot_general(
            a, b, (((1,), (1,)), ((), ())), preferred_element_type=jnp.float32
        )

    return product(x_high, high) + (product(x_high, low) + product(x_low, high))


def decode_rows(chunk):
    scales = chunk[PAIR:, :]
    return jnp.concatenate(
        [decode(chunk[b * BLK : (b + 1) * BLK, :], scales, b) for b in range(2)], axis=0
    )


def factor_kernel(
    sizes, layout, strip_in, pivot_any, strip_all,
    lower_out, high_out, small_out, low_out,
    near, pivot, whole, diagonal, load_sem, pivot_send, pivot_recv, near_send, near_recv, near_keep,
    strip_send, strip_recv,
):
    cubes, rows, cols = sizes
    range_rows, range_cols = layout[:2]
    cube, row, col = lax.axis_index("cube"), lax.axis_index("row"), lax.axis_index("col")
    strips, nears = strip_all.shape[0], near.shape[0]
    upper = [i * PB + j for i in range(PB) for j in range(i, PB)]
    root = (cube == 0) & (row == 0) & (col == 0)

    @pl.when(root)
    def _():
        load = pltpu.make_async_copy(pivot_any, pivot, load_sem.at[0])
        load.start()
        load.wait()

    greet_all(sizes)

    place = ring_position(row, rows)
    half = rows // 2
    ahead, behind = ring_member(place + 1, rows), ring_member(place - 1, rows)
    back = (place + rows - 1) % rows
    children = [
        ((cube == 0) & (row == 0) & (col < cols - 1), (0, 0, col + 1)),
        ((cube == 0) & (place < half), (0, ahead, col)),
        ((cube == 0) & ((place == 0) | (place > half)) & (back > half), (0, behind, col)),
    ] + [(cube == 0, (other, row, col)) for other in range(1, cubes)]

    def pivot_copy(block, child):
        return send(
            pivot.at[block],
            pivot.at[block],
            pivot_send.at[block, child],
            pivot_recv.at[block],
            children[child][1],
        )

    for block in upper:

        @pl.when(jnp.logical_not(root))
        def _():
            pivot_copy(block, 0).wait_recv()

        for child, (active, _) in enumerate(children):

            @pl.when(active)
            def _():
                pivot_copy(block, child).start()

    whole[...] = jnp.zeros_like(whole)
    for i in range(PB):
        for j in range(i, PB):
            whole[i * BLK : (i + 1) * BLK, j * BLK : (j + 1) * BLK] = pivot[i * PB + j]
        eye = lax.broadcasted_iota(jnp.int32, (BLK, BLK), 0) == lax.broadcasted_iota(
            jnp.int32, (BLK, BLK), 1
        )
        whole[i * BLK : (i + 1) * BLK, PANEL + i * BLK : PANEL + (i + 1) * BLK] = eye.astype(
            jnp.float32
        )

    first = (cube * cols + col) * range_cols
    owner_place = ring_position(first // range_rows, rows)
    first_chunk = (first % range_rows) // 2
    ring_dist = (place - owner_place + rows) % rows
    dists = (ring_dist, (rows - ring_dist) % rows)
    nexts = (ahead, behind)
    owner = ring_dist == 0

    def near_copy(index, way, at_owner):
        return send(
            strip_all.at[first_chunk + index] if at_owner else near.at[index],
            near.at[index],
            near_send.at[index],
            near_recv.at[index],
            (cube, nexts[way], col),
        )

    def near_stay(index):
        return pltpu.make_async_copy(
            strip_all.at[first_chunk + index], near.at[index], near_keep.at[index]
        )

    strip_active = [(cube == 0) & (col < cols - 1)] + [cube == 0] * (cubes - 1)
    strip_got = (cube > 0) | (col > 0)

    def strip_copy(index, child):
        device = (0, row, col + 1) if child == 0 else (child, row, col)
        return send(
            strip_all.at[index], strip_all.at[index], strip_send.at[index, child],
            strip_recv.at[index], device,
        )

    turns = strips + cols + rows
    each = -(-PB * SUBS // turns)

    def turn(time, carry):
        lag = col + jnp.where(cube > 0, 1, 0)
        index = time - lag
        ready = (index >= 0) & (index < strips)
        index = jnp.clip(index, 0, strips - 1)

        @pl.when(ready & strip_got)
        def _():
            strip_copy(index, 0).wait_recv()

        for child, active in enumerate(strip_active):

            @pl.when(ready & active)
            def _():
                strip_copy(index, child).start()

        for way in range(2):
            step = time - lag - first_chunk - dists[way]
            due = (step >= 0) & (step < nears) & ((step + 2 * rows + nears) % 2 == way)
            chunk = jnp.clip(step, 0, nears - 1)

            @pl.when(due & jnp.logical_not(owner))
            def _():
                near_copy(chunk, way, False).wait_recv()

            @pl.when(due & jnp.logical_not(owner) & (dists[way] < rows - 1))
            def _():
                near_copy(chunk, way, False).start()

            @pl.when(due & owner)
            def _():
                near_copy(chunk, way, True).start()
                near_stay(chunk).start()

        def advance(sub, inner):
            step = time * each + sub
            block = step // SUBS

            @pl.when(step < PB * SUBS)
            def _():
                @pl.when(step % SUBS == 0)
                def _():
                    start_block(block, whole, diagonal)

                eliminate_rows(step % SUBS, diagonal)

                @pl.when(step % SUBS == SUBS - 1)
                def _():
                    finish_block(block, whole, diagonal)

            return inner

        lax.fori_loop(0, each, advance, 0)
        return carry

    lax.fori_loop(0, turns, turn, 0)

    high_out[...], small_out[...] = split(whole[:, PANEL:])
    lower_out[...] = jnp.zeros_like(lower_out)
    for i in range(PB):
        for j in range(i + 1):
            block = whole[j * BLK : (j + 1) * BLK, i * BLK : (i + 1) * BLK].T
            if i == j:
                keep = lax.broadcasted_iota(jnp.int32, (BLK, BLK), 0) >= lax.broadcasted_iota(
                    jnp.int32, (BLK, BLK), 1
                )
                block = jnp.where(keep, block, 0.0)
            lower_out[i * BLK : (i + 1) * BLK, j * BLK : (j + 1) * BLK] = block

    @pl.when(owner)
    def _():
        def kept(index, carry):
            near_stay(index).wait()
            return carry

        lax.fori_loop(0, nears, kept, 0)

    def solve(index, carry):
        solved = times_transposed(decode_rows(near.at[index]), high_out[...], small_out[...])
        low_out[pl.ds(pl.multiple_of(index * PAIR, PAIR), PAIR), :] = solved.astype(low_out.dtype)
        return carry

    lax.fori_loop(0, nears, solve, 0)

    for block in upper:
        for child, (active, _) in enumerate(children):

            @pl.when(active)
            def _():
                pivot_copy(block, child).wait_send()

    def strips_sent(index, carry):
        for child, active in enumerate(strip_active):

            @pl.when(active)
            def _():
                strip_copy(index, child).wait_send()

        return carry

    lax.fori_loop(0, strips, strips_sent, 0)

    def nears_sent(index, carry):
        for way in range(2):

            @pl.when((index % 2 == way) & owner)
            def _():
                near_copy(index, way, True).wait_send()

            @pl.when((index % 2 == way) & jnp.logical_not(owner) & (dists[way] < rows - 1))
            def _():
                near_copy(index, way, False).wait_send()

        return carry

    lax.fori_loop(0, nears, nears_sent, 0)


def factor(strip, pivot, sizes, layout):
    cubes = sizes[0]
    range_cols = layout[1]
    square = (PANEL, PANEL)
    nears = range_cols // 2
    return pl.pallas_call(
        functools.partial(factor_kernel, sizes, layout),
        out_shape=(
            jax.ShapeDtypeStruct(strip.shape, strip.dtype),
            jax.ShapeDtypeStruct(square, jnp.float32),
            jax.ShapeDtypeStruct(square, jnp.bfloat16),
            jax.ShapeDtypeStruct(square, jnp.bfloat16),
            jax.ShapeDtypeStruct((range_cols * BLK, PANEL), jnp.bfloat16),
        ),
        in_specs=[ANY, ANY],
        out_specs=(ANY, VMEM, VMEM, VMEM, VMEM),
        input_output_aliases={0: 0},
        scratch_shapes=[
            pltpu.VMEM((nears,) + strip.shape[1:], strip.dtype),
            pltpu.VMEM(pivot.shape, pivot.dtype),
            pltpu.VMEM((PANEL, 2 * PANEL), jnp.float32),
            pltpu.VMEM((BLK, 2 * BLK), jnp.float32),
            pltpu.SemaphoreType.DMA((1,)),
            pltpu.SemaphoreType.DMA((PB * PB, 2 + cubes)),
            pltpu.SemaphoreType.DMA((PB * PB,)),
            pltpu.SemaphoreType.DMA((nears,)),
            pltpu.SemaphoreType.DMA((nears,)),
            pltpu.SemaphoreType.DMA((nears,)),
            pltpu.SemaphoreType.DMA((strip.shape[0], cubes)),
            pltpu.SemaphoreType.DMA((strip.shape[0],)),
        ],
        compiler_params=pltpu.CompilerParams(
            collective_id=1, has_side_effects=True, vmem_limit_bytes=50 * 2**20
        ),
        name="factor",
    )(strip, pivot)


def final_kernel(
    layout, tables, parent, strip, lower, high, small, low, arrived, schur, panel, solved, units
):
    range_rows, range_cols, row_cap, col_cap = layout
    children, groups, others = arrived.shape[:3]
    step = pl.program_id(0)
    base = children * (range_rows + range_cols)
    first_row, first_col = tables[base], tables[base + 1]

    @pl.when(step == 0)
    def _():
        def read(index, carry):
            at = (index // (groups * others), (index // others) % groups, index % others)
            for rank in range(col_cap):
                scales = arrived[at + (rank, slice(row_cap * BLK, None), slice(None))]
                scales = scales.astype(jnp.int32).astype(jnp.float32)
                units[at + (rank,)] = jnp.exp(scales * (1.0 / STEPS_PER_E))
            return carry

        lax.fori_loop(0, children * groups * others, read, 0)

    solved[...] = times_transposed(decode_rows(strip.at[0]), high[...], small[...])

    @pl.when(first_row + 2 * step < PB)
    def _():
        solved[...] = lower[...]

    panel[...] = solved[...]
    left = solved[...].astype(jnp.bfloat16)
    for chunk in range(range_cols // PB):
        at = slice(chunk * PANEL, (chunk + 1) * PANEL)
        product = lax.dot_general(
            left, low[at, :], (((1,), (1,)), ((), ())), preferred_element_type=jnp.float32
        )
        keep = first_row + 2 * step >= PB
        if chunk == 0:
            keep = keep & (first_col >= PB)
        schur[:, at] = jnp.where(keep, parent[:, at].astype(jnp.float32) - product, 0.0)
    for half in range(2):
        row_block = 2 * step + half
        rows = slice(half * BLK, (half + 1) * BLK)
        for child in range(children):
            row_slot = tables[child * range_rows + row_block]

            @pl.when((row_slot >= 0) & (first_row + row_block >= PB))
            def _():
                group, block = row_slot // row_cap, row_slot % row_cap
                high_at = pl.ds(pl.multiple_of(block * BLK, BLK), BLK)
                for slot in range(others * col_cap):
                    place = (child, group, slot // col_cap, slot % col_cap)
                    to = tables[base + 2 + child * others * col_cap + slot]
                    wanted = (to >= 0) & (first_col + to >= PB)
                    at = pl.ds(pl.multiple_of(jnp.maximum(to, 0) * BLK, BLK), BLK)
                    unit = units[place + (pl.ds(block, 1), slice(None))]
                    unit = unit * jnp.where(wanted, 1.0, 0.0)
                    codes = arrived[place + (high_at, slice(None))]
                    schur[rows, at] += codes.astype(jnp.int32).astype(jnp.float32) * unit


def final(tables, parent, strip, lower, high, small, low, arrived, layout):
    height, width = parent.shape
    return pl.pallas_call(
        functools.partial(final_kernel, layout),
        out_shape=(
            jax.ShapeDtypeStruct((height, width), jnp.float32),
            jax.ShapeDtypeStruct((height, PANEL), jnp.float32),
        ),
        grid_spec=pltpu.PrefetchScalarGridSpec(
            num_scalar_prefetch=1,
            grid=(height // PAIR,),
            in_specs=[
                pl.BlockSpec((PAIR, width), lambda s, t: (s, 0)),
                pl.BlockSpec((1,) + strip.shape[1:], lambda s, t: (s, 0, 0)),
                pl.BlockSpec((PAIR, PANEL), lambda s, t: (jnp.minimum(s, PANEL // PAIR - 1), 0)),
                VMEM,
                VMEM,
                VMEM,
                VMEM,
            ],
            out_specs=(
                pl.BlockSpec((PAIR, width), lambda s, t: (s, 0)),
                pl.BlockSpec((PAIR, PANEL), lambda s, t: (s, 0)),
            ),
            scratch_shapes=[
                pltpu.VMEM((PAIR, PANEL), jnp.float32),
                pltpu.VMEM(arrived.shape[:4] + (SCALE_ROWS, BLK), jnp.float32),
            ],
        ),
        compiler_params=pltpu.CompilerParams(vmem_limit_bytes=50 * 2**20),
        name="final",
    )(tables, parent, strip, lower, high, small, low, arrived)


def body(child_update, child_panel, parent_front, block_map):
    rows = lax.axis_size("row")
    cubes = lax.axis_size("cube")
    cols = lax.axis_size("col")
    ranges = cubes * cols
    child_index = lax.axis_index("cube")
    row_index = lax.axis_index("row")
    col_index = lax.axis_index("col")
    range_index = lax.axis_index(("cube", "col"))
    group_blocks = child_update.shape[1] // BLK
    row_cap = group_blocks // rows
    col_cap = max(1, group_blocks // ranges)
    range_rows = parent_front.shape[0] // BLK
    range_cols = parent_front.shape[1] // BLK

    children = block_map.shape[0]
    grouped = block_map.reshape(children, rows, group_blocks)
    row_dest = grouped // range_rows
    col_dest = grouped // range_cols
    row_slot = row_dest * row_cap + group_ranks(row_dest)
    col_rank = group_ranks(col_dest)
    row_rank = row_slot - row_dest * row_cap
    col_slot = col_dest * col_cap + col_rank
    my_rows = member_of_slot(row_slot[child_index, row_index], group_blocks, group_blocks)
    my_cols = member_of_slot(col_slot[child_index, col_index], ranges * col_cap, group_blocks)
    from_rows = slot_of_block(grouped, row_rank, row_cap, row_index * range_rows, range_rows)
    from_cols = slot_of_block(grouped, col_rank, col_cap, range_index * range_cols, range_cols)
    local = grouped - range_index * range_cols
    inside = (local >= 0) & (local < range_cols)
    at_rank = col_rank[..., None] == jnp.arange(col_cap)
    to_cols = jnp.sum(jnp.where(inside[..., None] & at_rank, local[..., None] + 1, 0), axis=2) - 1
    tables = jnp.concatenate(
        [
            from_rows.reshape(-1),
            from_cols.reshape(-1),
            jnp.stack([row_index * range_rows, range_index * range_cols]),
            to_cols.reshape(-1),
        ]
    ).astype(jnp.int32)

    arrived = contribute(
        child_panel[0], child_update[0], my_rows, my_cols, (cubes, rows, cols, row_cap, col_cap)
    )
    layout = (range_rows, range_cols, row_cap, col_cap)
    strip, pivot = assemble(tables, arrived, parent_front, layout)
    strip, lower, high, small, low = factor(strip, pivot, (cubes, rows, cols), layout)
    return final(tables, parent_front, strip, lower, high, small, low, arrived, layout)


def solution(mesh):
    placed = (P("cube", "row", "col"), P("cube", "row", None), P("row", ("cube", "col")), P())
    return jax.shard_map(
        body,
        mesh=mesh,
        in_specs=placed,
        out_specs=(P("row", ("cube", "col")), P("row", None)),
        check_vma=False,
    )
```

```python
import functools
import math

import jax
import jax.numpy as jnp
from jax import lax
from jax.experimental import pallas as pl
from jax.experimental.pallas import tpu as pltpu
from jax.sharding import PartitionSpec as P

BLK = 128
PANEL = 512
PB = PANEL // BLK
PAIR = 2 * BLK
SCALE_ROWS = 16
TOP = 32700.0
STEPS_PER_E = 64.0 / math.log(2.0)
HIGHEST = lax.Precision.HIGHEST
MESH = pl.DeviceIdType.MESH
ANY = pl.BlockSpec(memory_space=pl.ANY)
VMEM = pl.BlockSpec(memory_space=pltpu.VMEM)
SMEM = pl.BlockSpec(memory_space=pltpu.SMEM)


def group_ranks(labels):
    position = jnp.arange(labels.shape[-1])
    before = position[:, None] > position[None, :]
    same_label = labels[..., :, None] == labels[..., None, :]
    return jnp.sum(jnp.logical_and(same_label, before), axis=-1)


def member_of_slot(slot, slots, count):
    hits = (slot[:, None] == jnp.arange(slots)).astype(jnp.int32)
    return jnp.sum(hits * jnp.arange(count, dtype=jnp.int32)[:, None], axis=0)


def slot_of_block(grouped, slot_in_group, cap, first, count):
    groups = grouped.shape[1]
    wanted = first + jnp.arange(count, dtype=jnp.int32)
    hits = grouped[..., None] == wanted
    value = jnp.arange(groups, dtype=jnp.int32)[None, :, None] * cap + slot_in_group
    total = jnp.sum(jnp.where(hits, value[..., None] + 1, 0), axis=(1, 2))
    return total.astype(jnp.int32) - 1


def encode(x):
    peak = jnp.max(jnp.abs(x), axis=0, keepdims=True)
    unit = jnp.ceil(jnp.log(jnp.maximum(peak, 1e-30) * (1.0 / TOP)) * STEPS_PER_E)
    codes = jnp.round(x * jnp.exp(unit * (-1.0 / STEPS_PER_E)))
    return codes.astype(jnp.int32).astype(jnp.int16), unit


def scale_tile(units):
    width = units[0].shape[-1]
    row = lax.broadcasted_iota(jnp.int32, (SCALE_ROWS, width), 0)
    tile = jnp.zeros((SCALE_ROWS, width), jnp.float32)
    for index, unit in enumerate(units):
        tile = jnp.where(row == index, unit, tile)
    return tile.astype(jnp.int32).astype(jnp.int16)


def decode(codes, scales, index):
    scales = scales.astype(jnp.int32).astype(jnp.float32)
    row = lax.broadcasted_iota(jnp.int32, scales.shape, 0)
    unit = jnp.sum(jnp.where(row == index, scales, 0.0), axis=0, keepdims=True)
    return codes.astype(jnp.int32).astype(jnp.float32) * jnp.exp(unit * (1.0 / STEPS_PER_E))


def ring_position(index, count):
    odd = index % 2
    return (1 - odd) * (index // 2) + odd * (count - 1 - index // 2)


def ring_member(position, count):
    position = (position + count) % count
    back = position // (count // 2)
    return (1 - back) * (2 * position) + back * (2 * (count - 1 - position) + 1)


def greet_all(sizes):
    cubes, rows, cols = sizes
    count = cubes * rows * cols
    me = (lax.axis_index("cube") * rows + lax.axis_index("row")) * cols + lax.axis_index("col")
    barrier = pltpu.get_barrier_semaphore()

    def greet(step, carry):
        other = (me + step) % count
        device = (other // (rows * cols), (other // cols) % rows, other % cols)
        pl.semaphore_signal(barrier, inc=1, device_id=device, device_id_type=MESH)
        return carry

    lax.fori_loop(1, count, greet, 0)
    pl.semaphore_wait(barrier, count - 1)
    return me


def send(src, dst, send_sem, recv_sem, device):
    return pltpu.make_async_remote_copy(
        src_ref=src,
        dst_ref=dst,
        send_sem=send_sem,
        recv_sem=recv_sem,
        device_id=device,
        device_id_type=MESH,
    )


def pair_at(time, pairs, col):
    return ((pairs - 1) * time + col + 3) % pairs


def contribute_kernel(
    sizes, tables, own_any, update_any, arrived, own, column, update, product, packed,
    load_sem, pass_send, pass_recv, out_send, out_recv, keep_sem,
):
    cubes, rows, cols, row_cap, col_cap = sizes
    cube, row, col = lax.axis_index("cube"), lax.axis_index("row"), lax.axis_index("col")
    slots = cubes * cols * col_cap
    pairs = slots // 2
    together = min(2, col_cap)
    group_blocks = own.shape[0]
    col_blocks = update.shape[0]
    tile = min(PB, group_blocks)

    def load_update(block):
        left = pl.multiple_of(block * BLK, BLK)
        return pltpu.make_async_copy(
            update_any.at[:, :, pl.ds(left, BLK)], update.at[block], load_sem.at[1 + block]
        )

    load_own = pltpu.make_async_copy(own_any, own, load_sem.at[0])
    load_own.start()

    def start_load(block, carry):
        load_update(block).start()
        return carry

    lax.fori_loop(0, col_blocks, start_load, 0)
    me = greet_all((cubes, rows, cols))
    load_own.wait()

    place = ring_position(row, rows)
    forward_dist = (place - ring_position(col, rows) + rows) % rows
    dists = (forward_dist, (rows - forward_dist) % rows)
    nexts = (ring_member(place + 1, rows), ring_member(place - 1, rows))

    @pl.when(row == col)
    def _():
        def fill(slot, carry):
            column[slot] = own[tables[group_blocks + slot]]
            return carry

        lax.fori_loop(0, slots, fill, 0)

    def passing(slot, way):
        return send(
            column.at[slot],
            column.at[slot],
            pass_send.at[slot],
            pass_recv.at[slot],
            (cube, nexts[way], col),
        )

    def destination(slot, other_row):
        target = slot // col_cap
        return (target // cols, other_row, target % cols)

    def outgoing(slot, other_row):
        return send(
            packed.at[pl.ds(slot, together), other_row],
            arrived.at[cube, row, col, pl.ds(slot % col_cap, together)],
            out_send.at[slot // together, other_row],
            out_recv.at[me, (slot % col_cap) // together],
            destination(slot, other_row),
        )

    def staying(slot, other_row):
        return pltpu.make_async_copy(
            packed.at[pl.ds(slot, together), other_row],
            arrived.at[cube, row, col, pl.ds(slot % col_cap, together)],
            keep_sem.at[(slot % col_cap) // together],
        )

    def is_mine(slot, other_row):
        to_cube, to_row, to_col = destination(slot, other_row)
        return (to_cube == cube) & (to_row == row) & (to_col == col)

    def work(time):
        pair = pair_at(time, pairs, col)
        panel = column[pl.ds(2 * pair, 2)].reshape(PAIR, own.shape[2])

        def multiply(step, carry):
            at = pl.ds(step * tile, tile)
            product[at] = lax.dot_general(
                own[at].reshape(tile * BLK, own.shape[2]),
                panel,
                (((1,), (1,)), ((), ())),
                preferred_element_type=jnp.float32,
            ).reshape(tile, BLK, PAIR)
            return carry

        lax.fori_loop(0, group_blocks // tile, multiply, 0)

        def pack(step, carry):
            other_row = (row + 1 + step) % rows
            for half in range(2):
                slot = 2 * pair + half
                left = tables[group_blocks + slot]
                units = []
                for block in range(row_cap):
                    high = tables[other_row * row_cap + block]
                    value = update[left, high] - product[high, :, half * BLK : (half + 1) * BLK]
                    codes, unit = encode(value)
                    packed[slot, other_row, block * BLK : (block + 1) * BLK, :] = codes
                    units.append(unit)
                packed[slot, other_row, row_cap * BLK :, :] = scale_tile(units)
            for part in range(2 // together):
                slot = 2 * pair + part * together
                mine = is_mine(slot, other_row)

                @pl.when(mine)
                def _():
                    staying(slot, other_row).start()

                @pl.when(jnp.logical_not(mine))
                def _():
                    outgoing(slot, other_row).start()

            return carry

        lax.fori_loop(0, rows, pack, 0)

    def turn(time, carry):
        for way in range(2):
            step = time - dists[way]
            ready = (step >= 0) & (step < pairs)
            slot = 2 * pair_at(jnp.clip(step, 0, pairs - 1), pairs, col) + way

            @pl.when(ready & (dists[way] > 0))
            def _():
                passing(slot, way).wait_recv()

            @pl.when(ready & (dists[way] < rows - 1))
            def _():
                passing(slot, way).start()

        @pl.when(time == rows - 1)
        def _():
            def end_load(block, inner):
                load_update(block).wait()
                return inner

            lax.fori_loop(0, col_blocks, end_load, 0)

        @pl.when(time >= rows - 1)
        def _():
            work(jnp.maximum(time - (rows - 1), 0))

        return carry

    lax.fori_loop(0, pairs + rows - 1, turn, 0)

    for way in range(2):

        @pl.when(dists[way] < rows - 1)
        def _():
            def sent(pair, carry):
                passing(2 * pair + way, way).wait_send()
                return carry

            lax.fori_loop(0, pairs, sent, 0)

    def settle(index, carry):
        slot = (index // rows) * together
        other_row = index % rows
        mine = is_mine(slot, other_row)

        @pl.when(mine)
        def _():
            staying(slot, other_row).wait()

        @pl.when(jnp.logical_not(mine))
        def _():
            outgoing(slot, other_row).wait_send()

        return carry

    lax.fori_loop(0, (slots // together) * rows, settle, 0)

    count = cubes * rows * cols

    def collect(index, carry):
        other = (me + index) % count
        device = (other // (rows * cols), (other // cols) % rows, other % cols)
        for part in range(col_cap // together):
            send(
                packed.at[pl.ds(0, together), 0],
                arrived.at[
                    device[0], device[1], device[2], part * together : (part + 1) * together
                ],
                out_send.at[0, 0],
                out_recv.at[other, part],
                device,
            ).wait_recv()
        return carry

    lax.fori_loop(1, count, collect, 0)


def contribute(own_panel, update, my_rows, my_cols, sizes):
    cubes, rows, cols, row_cap, col_cap = sizes
    slots = cubes * cols * col_cap
    together = min(2, col_cap)
    depth = own_panel.shape[1]
    high, wide = update.shape[0] // BLK, update.shape[1] // BLK
    piece = row_cap * BLK + SCALE_ROWS
    tables = jnp.concatenate([my_rows, my_cols]).astype(jnp.int32)
    return pl.pallas_call(
        functools.partial(contribute_kernel, sizes),
        out_shape=jax.ShapeDtypeStruct((cubes, rows, cols, col_cap, piece, BLK), jnp.int16),
        in_specs=[SMEM, ANY, ANY],
        out_specs=ANY,
        scratch_shapes=[
            pltpu.VMEM((high, BLK, depth), own_panel.dtype),
            pltpu.VMEM((slots, BLK, depth), own_panel.dtype),
            pltpu.VMEM((wide, high, BLK, BLK), jnp.float32),
            pltpu.VMEM((high, BLK, PAIR), jnp.float32),
            pltpu.VMEM((slots, rows, piece, BLK), jnp.int16),
            pltpu.SemaphoreType.DMA((1 + wide,)),
            pltpu.SemaphoreType.DMA((slots,)),
            pltpu.SemaphoreType.DMA((slots,)),
            pltpu.SemaphoreType.DMA((slots // together, rows)),
            pltpu.SemaphoreType.DMA((cubes * rows * cols, col_cap // together)),
            pltpu.SemaphoreType.DMA((col_cap // together,)),
        ],
        compiler_params=pltpu.CompilerParams(
            collective_id=0, has_side_effects=True, vmem_limit_bytes=56 * 2**20
        ),
        name="contribute",
    )(tables, own_panel.reshape(high, BLK, depth), update.reshape(high, BLK, wide * BLK))


def arrivals(layout, tables, arrived, row_block, col_block):
    range_rows, range_cols, row_cap, col_cap = layout
    children = arrived.shape[0]
    found = []
    for child in range(children):
        row_slot = tables[child * range_rows + row_block]
        col_slot = tables[children * range_rows + child * range_cols + col_block]
        row_at, col_at = jnp.maximum(row_slot, 0), jnp.maximum(col_slot, 0)
        place = (child, row_at // row_cap, col_at // col_cap, col_at % col_cap)
        block = row_at % row_cap

        def piece(place=place, block=block):
            codes = arrived[place + (pl.ds(pl.multiple_of(block * BLK, BLK), BLK), slice(None))]
            scales = arrived[place + (pl.ds(row_cap * BLK, SCALE_ROWS), slice(None))]
            return decode(codes, scales, block)

        found.append(((row_slot >= 0) & (col_slot >= 0), piece))
    return found


def assemble_kernel(layout, tables, arrived, parent_any, strip_out, pivot_out, strip, total, sem):
    range_rows = layout[0]
    load = pltpu.make_async_copy(parent_any.at[:, pl.ds(0, PANEL)], strip, sem.at[0])
    load.start()
    load.wait()

    def strip_rows(step, carry):
        tile = jnp.zeros((SCALE_ROWS, PANEL), jnp.float32)
        for half in range(2):
            row_block = 2 * step + half
            high = pl.multiple_of(row_block * BLK, BLK)
            total[...] = strip[pl.ds(high, BLK), :].astype(jnp.float32)
            for block in range(PB):
                at = slice(block * BLK, (block + 1) * BLK)
                for valid, piece in arrivals(layout, tables, arrived, row_block, block):

                    @pl.when(valid)
                    def _(piece=piece):
                        total[:, at] += piece()

            codes, unit = encode(total[...])
            strip_out[step, half * BLK : (half + 1) * BLK, :] = codes
            row = lax.broadcasted_iota(jnp.int32, (SCALE_ROWS, PANEL), 0)
            tile = jnp.where(row == half, unit, tile)
            for block in range(PB):

                @pl.when(row_block == block)
                def _():
                    for other in range(block, PB):
                        pivot_out[block * PB + other] = total[:, other * BLK : (other + 1) * BLK]

        strip_out[step, PAIR:, :] = tile.astype(jnp.int32).astype(jnp.int16)
        return carry

    lax.fori_loop(0, range_rows // 2, strip_rows, 0)


def assemble(tables, arrived, parent, layout):
    range_rows = layout[0]
    return pl.pallas_call(
        functools.partial(assemble_kernel, layout),
        out_shape=(
            jax.ShapeDtypeStruct((range_rows // 2, PAIR + SCALE_ROWS, PANEL), jnp.int16),
            jax.ShapeDtypeStruct((PB * PB, BLK, BLK), jnp.float32),
        ),
        in_specs=[SMEM, VMEM, ANY],
        out_specs=(VMEM, VMEM),
        scratch_shapes=[
            pltpu.VMEM((range_rows * BLK, PANEL), parent.dtype),
            pltpu.VMEM((BLK, PANEL), jnp.float32),
            pltpu.SemaphoreType.DMA((1,)),
        ],
        compiler_params=pltpu.CompilerParams(vmem_limit_bytes=50 * 2**20),
        name="assemble",
    )(tables, arrived, parent)


SUB = 8
SUBS = BLK // SUB


def terms(x):
    first = x.astype(jnp.bfloat16).astype(jnp.float32)
    second = (x - first).astype(jnp.bfloat16).astype(jnp.float32)
    return first, second, x - first - second


def dot_full(a, b):
    a1, a2, a3 = terms(a)
    b1, b2, b3 = terms(b)
    left = jnp.concatenate([a1, a1, a2, a1, a2, a3], axis=0).astype(jnp.bfloat16)
    right = jnp.concatenate([b1, b2, b1, b3, b2, b1], axis=0).astype(jnp.bfloat16)
    return lax.dot_general(
        left, right, (((0,), (0,)), ((), ())), preferred_element_type=jnp.float32
    )


def eliminate_rows(step, diagonal):
    at = pl.ds(pl.multiple_of(step * SUB, SUB), SUB)
    block = diagonal[at, :]
    small = pltpu.roll(block[:, :BLK], (BLK - step * SUB) % BLK, 1)
    columns = [jnp.broadcast_to(small[:, j : j + 1], (SUB, BLK)) for j in range(SUB)]
    left = {
        (i, j): jnp.broadcast_to(columns[j][i : i + 1, :], (SUB, BLK))
        for j in range(SUB)
        for i in range(j, SUB)
    }
    done = [jnp.broadcast_to(block[i : i + 1, :], (SUB, 2 * BLK)) for i in range(SUB)]
    for k in range(SUB):
        pivot = left[k, k]
        root = lax.rsqrt(pivot)
        root = root * (1.5 - 0.5 * pivot * root * root)
        done[k] = done[k] * jnp.concatenate([root, root], axis=1)
        entries = {i: left[i, k] * root for i in range(k + 1, SUB)}
        for j in range(k + 1, SUB):
            for i in range(j, SUB):
                left[i, j] = left[i, j] - entries[i] * entries[j]
            wide = jnp.concatenate([entries[j], entries[j]], axis=1)
            done[j] = done[j] - wide * done[k]
    sub = lax.broadcasted_iota(jnp.int32, (SUB, 2 * BLK), 0)
    rows = done[0]
    for k in range(1, SUB):
        rows = jnp.where(sub == k, done[k], rows)
    diagonal[at, :] = rows
    lane = lax.broadcasted_iota(jnp.int32, (SUB, BLK), 1)
    below = jnp.where(lane >= (step + 1) * SUB, rows[:, :BLK], 0.0)
    diagonal[...] -= dot_full(below, rows)


def finish_block(block, whole, diagonal):
    at = pl.ds(pl.multiple_of(block * BLK, BLK), BLK)
    window = pl.ds(pl.multiple_of((block + 1) * BLK, BLK), PANEL)
    solved = jnp.dot(
        diagonal[:, BLK:], whole[at, window], precision=HIGHEST, preferred_element_type=jnp.float32
    )
    whole[at, at] = diagonal[:, :BLK]
    whole[at, window] = solved
    for below in range(1, PB):

        @pl.when(below > block)
        def _():
            whole[below * BLK : (below + 1) * BLK, window] -= dot_full(
                whole[at, below * BLK : (below + 1) * BLK], whole[at, window]
            )


def start_block(block, whole, diagonal):
    at = pl.ds(pl.multiple_of(block * BLK, BLK), BLK)
    diagonal[:, :BLK] = whole[at, at]
    eye = lax.broadcasted_iota(jnp.int32, (BLK, BLK), 0) == lax.broadcasted_iota(
        jnp.int32, (BLK, BLK), 1
    )
    diagonal[:, BLK:] = eye.astype(jnp.float32)


def split(x):
    high = x.astype(jnp.bfloat16)
    return high, (x - high.astype(jnp.float32)).astype(jnp.bfloat16)


def times_transposed(x, high, low):
    x_high, x_low = split(x)

    def product(a, b):
        return lax.dot_general(
            a, b, (((1,), (1,)), ((), ())), preferred_element_type=jnp.float32
        )

    return product(x_high, high) + (product(x_high, low) + product(x_low, high))


def decode_rows(chunk):
    scales = chunk[PAIR:, :]
    return jnp.concatenate(
        [decode(chunk[b * BLK : (b + 1) * BLK, :], scales, b) for b in range(2)], axis=0
    )


def factor_kernel(
    sizes, layout, strip_in, pivot_any, strip_all,
    lower_out, high_out, small_out, low_out,
    near, pivot, whole, diagonal, load_sem, pivot_send, pivot_recv, near_send, near_recv, near_keep,
    strip_send, strip_recv,
):
    cubes, rows, cols = sizes
    range_rows, range_cols = layout[:2]
    cube, row, col = lax.axis_index("cube"), lax.axis_index("row"), lax.axis_index("col")
    strips, nears = strip_all.shape[0], near.shape[0]
    upper = [i * PB + j for i in range(PB) for j in range(i, PB)]
    root = (cube == 0) & (row == 0) & (col == 0)

    @pl.when(root)
    def _():
        load = pltpu.make_async_copy(pivot_any, pivot, load_sem.at[0])
        load.start()
        load.wait()

    greet_all(sizes)

    place = ring_position(row, rows)
    half = rows // 2
    ahead, behind = ring_member(place + 1, rows), ring_member(place - 1, rows)
    back = (place + rows - 1) % rows
    children = [
        ((cube == 0) & (row == 0) & (col < cols - 1), (0, 0, col + 1)),
        ((cube == 0) & (place < half), (0, ahead, col)),
        ((cube == 0) & ((place == 0) | (place > half)) & (back > half), (0, behind, col)),
    ] + [(cube == 0, (other, row, col)) for other in range(1, cubes)]

    def pivot_copy(block, child):
        return send(
            pivot.at[block],
            pivot.at[block],
            pivot_send.at[block, child],
            pivot_recv.at[block],
            children[child][1],
        )

    near_ring = jnp.minimum(place, rows - place)
    depth = col + near_ring + jnp.where(cube > 0, 1, 0)
    batch = 4
    pivot_turns = -(-len(upper) // batch) + (cols - 1) + rows // 2 + 1

    def pass_pivot(blocks):
        for block in blocks:

            @pl.when(jnp.logical_not(root))
            def _():
                pivot_copy(block, 0).wait_recv()

            for child, (active, _) in enumerate(children):

                @pl.when(active)
                def _():
                    pivot_copy(block, child).start()

    def set_whole():
        whole[...] = jnp.zeros_like(whole)
        for i in range(PB):
            for j in range(i, PB):
                whole[i * BLK : (i + 1) * BLK, j * BLK : (j + 1) * BLK] = pivot[i * PB + j]
            eye = lax.broadcasted_iota(jnp.int32, (BLK, BLK), 0) == lax.broadcasted_iota(
                jnp.int32, (BLK, BLK), 1
            )
            whole[i * BLK : (i + 1) * BLK, PANEL + i * BLK : PANEL + (i + 1) * BLK] = eye.astype(
                jnp.float32
            )

    first = (cube * cols + col) * range_cols
    owner_place = ring_position(first // range_rows, rows)
    first_chunk = (first % range_rows) // 2
    sections = strips // nears
    section = first_chunk // nears
    ring_dist = (place - owner_place + rows) % rows
    dists = (ring_dist, (rows - ring_dist) % rows)
    nexts = (ahead, behind)
    owner = ring_dist == 0

    def near_copy(index, way, at_owner):
        return send(
            strip_all.at[first_chunk + index] if at_owner else near.at[index],
            near.at[index],
            near_send.at[index],
            near_recv.at[index],
            (cube, nexts[way], col),
        )

    def near_stay(index):
        return pltpu.make_async_copy(
            strip_all.at[first_chunk + index], near.at[index], near_keep.at[index]
        )

    strip_active = [(cube == 0) & (col < cols - 1)] + [cube == 0] * (cubes - 1)
    strip_got = (cube > 0) | (col > 0)

    def strip_copy(index, child):
        device = (0, row, col + 1) if child == 0 else (child, row, col)
        return send(
            strip_all.at[index], strip_all.at[index], strip_send.at[index, child],
            strip_recv.at[index], device,
        )

    turns = strips + cols + rows
    each = -(-PB * SUBS // (turns - pivot_turns))

    def turn(time, carry):
        for first_block in range(0, len(upper), batch):

            @pl.when(time == depth + first_block // batch)
            def _():
                pass_pivot(upper[first_block : first_block + batch])

        @pl.when(time == pivot_turns)
        def _():
            set_whole()

        lag = col + jnp.where(cube > 0, 1, 0)
        index = time - lag
        ready = (index >= 0) & (index < strips)
        index = jnp.clip(index, 0, strips - 1)
        index = (index % sections) * nears + index // sections

        @pl.when(ready & strip_got)
        def _():
            strip_copy(index, 0).wait_recv()

        for child, active in enumerate(strip_active):

            @pl.when(ready & active)
            def _():
                strip_copy(index, child).start()

        for way in range(2):
            step = time - lag - section - dists[way]
            late = jnp.clip(step, 0, strips - 1)
            chunk = late // sections
            due = (step >= 0) & (step < strips) & (late % sections == 0) & (chunk % 2 == way)

            @pl.when(due & jnp.logical_not(owner))
            def _():
                near_copy(chunk, way, False).wait_recv()

            @pl.when(due & jnp.logical_not(owner) & (dists[way] < rows - 1))
            def _():
                near_copy(chunk, way, False).start()

            @pl.when(due & owner)
            def _():
                near_copy(chunk, way, True).start()
                near_stay(chunk).start()

        def advance(sub, inner):
            step = (time - pivot_turns) * each + sub
            block = step // SUBS

            @pl.when((step >= 0) & (step < PB * SUBS))
            def _():
                @pl.when(step % SUBS == 0)
                def _():
                    start_block(block, whole, diagonal)

                eliminate_rows(step % SUBS, diagonal)

                @pl.when(step % SUBS == SUBS - 1)
                def _():
                    finish_block(block, whole, diagonal)

            return inner

        lax.fori_loop(0, each, advance, 0)
        return carry

    lax.fori_loop(0, turns, turn, 0)

    high_out[...], small_out[...] = split(whole[:, PANEL:])
    lower_out[...] = jnp.zeros_like(lower_out)
    for i in range(PB):
        for j in range(i + 1):
            block = whole[j * BLK : (j + 1) * BLK, i * BLK : (i + 1) * BLK].T
            if i == j:
                keep = lax.broadcasted_iota(jnp.int32, (BLK, BLK), 0) >= lax.broadcasted_iota(
                    jnp.int32, (BLK, BLK), 1
                )
                block = jnp.where(keep, block, 0.0)
            lower_out[i * BLK : (i + 1) * BLK, j * BLK : (j + 1) * BLK] = block

    @pl.when(owner)
    def _():
        def kept(index, carry):
            near_stay(index).wait()
            return carry

        lax.fori_loop(0, nears, kept, 0)

    def solve(index, carry):
        solved = times_transposed(decode_rows(near.at[index]), high_out[...], small_out[...])
        low_out[pl.ds(pl.multiple_of(index * PAIR, PAIR), PAIR), :] = solved.astype(low_out.dtype)
        return carry

    lax.fori_loop(0, nears, solve, 0)

    for block in upper:
        for child, (active, _) in enumerate(children):

            @pl.when(active)
            def _():
                pivot_copy(block, child).wait_send()

    def strips_sent(index, carry):
        for child, active in enumerate(strip_active):

            @pl.when(active)
            def _():
                strip_copy(index, child).wait_send()

        return carry

    lax.fori_loop(0, strips, strips_sent, 0)

    def nears_sent(index, carry):
        for way in range(2):

            @pl.when((index % 2 == way) & owner)
            def _():
                near_copy(index, way, True).wait_send()

            @pl.when((index % 2 == way) & jnp.logical_not(owner) & (dists[way] < rows - 1))
            def _():
                near_copy(index, way, False).wait_send()

        return carry

    lax.fori_loop(0, nears, nears_sent, 0)


def factor(strip, pivot, sizes, layout):
    cubes = sizes[0]
    range_cols = layout[1]
    square = (PANEL, PANEL)
    nears = range_cols // 2
    return pl.pallas_call(
        functools.partial(factor_kernel, sizes, layout),
        out_shape=(
            jax.ShapeDtypeStruct(strip.shape, strip.dtype),
            jax.ShapeDtypeStruct(square, jnp.float32),
            jax.ShapeDtypeStruct(square, jnp.bfloat16),
            jax.ShapeDtypeStruct(square, jnp.bfloat16),
            jax.ShapeDtypeStruct((range_cols * BLK, PANEL), jnp.bfloat16),
        ),
        in_specs=[ANY, ANY],
        out_specs=(ANY, VMEM, VMEM, VMEM, VMEM),
        input_output_aliases={0: 0},
        scratch_shapes=[
            pltpu.VMEM((nears,) + strip.shape[1:], strip.dtype),
            pltpu.VMEM(pivot.shape, pivot.dtype),
            pltpu.VMEM((PANEL, 2 * PANEL), jnp.float32),
            pltpu.VMEM((BLK, 2 * BLK), jnp.float32),
            pltpu.SemaphoreType.DMA((1,)),
            pltpu.SemaphoreType.DMA((PB * PB, 2 + cubes)),
            pltpu.SemaphoreType.DMA((PB * PB,)),
            pltpu.SemaphoreType.DMA((nears,)),
            pltpu.SemaphoreType.DMA((nears,)),
            pltpu.SemaphoreType.DMA((nears,)),
            pltpu.SemaphoreType.DMA((strip.shape[0], cubes)),
            pltpu.SemaphoreType.DMA((strip.shape[0],)),
        ],
        compiler_params=pltpu.CompilerParams(
            collective_id=1, has_side_effects=True, vmem_limit_bytes=50 * 2**20
        ),
        name="factor",
    )(strip, pivot)


def final_kernel(
    layout, tables, parent, strip, lower, high, small, low, arrived, schur, panel, solved, units
):
    range_rows, range_cols, row_cap, col_cap = layout
    children, groups, others = arrived.shape[:3]
    step = pl.program_id(0)
    base = children * (range_rows + range_cols)
    first_row, first_col = tables[base], tables[base + 1]

    @pl.when(step == 0)
    def _():
        def read(index, carry):
            at = (index // (groups * others), (index // others) % groups, index % others)
            for rank in range(col_cap):
                scales = arrived[at + (rank, slice(row_cap * BLK, None), slice(None))]
                scales = scales.astype(jnp.int32).astype(jnp.float32)
                units[at + (rank,)] = jnp.exp(scales * (1.0 / STEPS_PER_E))
            return carry

        lax.fori_loop(0, children * groups * others, read, 0)

    solved[...] = times_transposed(decode_rows(strip.at[0]), high[...], small[...])

    @pl.when(first_row + 2 * step < PB)
    def _():
        solved[...] = lower[...]

    panel[...] = solved[...]
    left = solved[...].astype(jnp.bfloat16)
    for chunk in range(range_cols // PB):
        at = slice(chunk * PANEL, (chunk + 1) * PANEL)
        product = lax.dot_general(
            left, low[at, :], (((1,), (1,)), ((), ())), preferred_element_type=jnp.float32
        )
        keep = first_row + 2 * step >= PB
        if chunk == 0:
            keep = keep & (first_col >= PB)
        schur[:, at] = jnp.where(keep, parent[:, at].astype(jnp.float32) - product, 0.0)
    for half in range(2):
        row_block = 2 * step + half
        rows = slice(half * BLK, (half + 1) * BLK)
        for child in range(children):
            row_slot = tables[child * range_rows + row_block]

            @pl.when((row_slot >= 0) & (first_row + row_block >= PB))
            def _():
                group, block = row_slot // row_cap, row_slot % row_cap
                high_at = pl.ds(pl.multiple_of(block * BLK, BLK), BLK)
                for slot in range(others * col_cap):
                    place = (child, group, slot // col_cap, slot % col_cap)
                    to = tables[base + 2 + child * others * col_cap + slot]
                    wanted = (to >= 0) & (first_col + to >= PB)
                    at = pl.ds(pl.multiple_of(jnp.maximum(to, 0) * BLK, BLK), BLK)
                    unit = units[place + (pl.ds(block, 1), slice(None))]
                    unit = unit * jnp.where(wanted, 1.0, 0.0)
                    codes = arrived[place + (high_at, slice(None))]
                    schur[rows, at] += codes.astype(jnp.int32).astype(jnp.float32) * unit


def final(tables, parent, strip, lower, high, small, low, arrived, layout):
    height, width = parent.shape
    return pl.pallas_call(
        functools.partial(final_kernel, layout),
        out_shape=(
            jax.ShapeDtypeStruct((height, width), jnp.float32),
            jax.ShapeDtypeStruct((height, PANEL), jnp.float32),
        ),
        grid_spec=pltpu.PrefetchScalarGridSpec(
            num_scalar_prefetch=1,
            grid=(height // PAIR,),
            in_specs=[
                pl.BlockSpec((PAIR, width), lambda s, t: (s, 0)),
                pl.BlockSpec((1,) + strip.shape[1:], lambda s, t: (s, 0, 0)),
                pl.BlockSpec((PAIR, PANEL), lambda s, t: (jnp.minimum(s, PANEL // PAIR - 1), 0)),
                VMEM,
                VMEM,
                VMEM,
                VMEM,
            ],
            out_specs=(
                pl.BlockSpec((PAIR, width), lambda s, t: (s, 0)),
                pl.BlockSpec((PAIR, PANEL), lambda s, t: (s, 0)),
            ),
            scratch_shapes=[
                pltpu.VMEM((PAIR, PANEL), jnp.float32),
                pltpu.VMEM(arrived.shape[:4] + (SCALE_ROWS, BLK), jnp.float32),
            ],
        ),
        compiler_params=pltpu.CompilerParams(vmem_limit_bytes=50 * 2**20),
        name="final",
    )(tables, parent, strip, lower, high, small, low, arrived)


def body(child_update, child_panel, parent_front, block_map):
    rows = lax.axis_size("row")
    cubes = lax.axis_size("cube")
    cols = lax.axis_size("col")
    ranges = cubes * cols
    child_index = lax.axis_index("cube")
    row_index = lax.axis_index("row")
    col_index = lax.axis_index("col")
    range_index = lax.axis_index(("cube", "col"))
    group_blocks = child_update.shape[1] // BLK
    row_cap = group_blocks // rows
    col_cap = max(1, group_blocks // ranges)
    range_rows = parent_front.shape[0] // BLK
    range_cols = parent_front.shape[1] // BLK

    children = block_map.shape[0]
    grouped = block_map.reshape(children, rows, group_blocks)
    row_dest = grouped // range_rows
    col_dest = grouped // range_cols
    row_slot = row_dest * row_cap + group_ranks(row_dest)
    col_rank = group_ranks(col_dest)
    row_rank = row_slot - row_dest * row_cap
    col_slot = col_dest * col_cap + col_rank
    my_rows = member_of_slot(row_slot[child_index, row_index], group_blocks, group_blocks)
    my_cols = member_of_slot(col_slot[child_index, col_index], ranges * col_cap, group_blocks)
    from_rows = slot_of_block(grouped, row_rank, row_cap, row_index * range_rows, range_rows)
    from_cols = slot_of_block(grouped, col_rank, col_cap, range_index * range_cols, range_cols)
    local = grouped - range_index * range_cols
    inside = (local >= 0) & (local < range_cols)
    at_rank = col_rank[..., None] == jnp.arange(col_cap)
    to_cols = jnp.sum(jnp.where(inside[..., None] & at_rank, local[..., None] + 1, 0), axis=2) - 1
    tables = jnp.concatenate(
        [
            from_rows.reshape(-1),
            from_cols.reshape(-1),
            jnp.stack([row_index * range_rows, range_index * range_cols]),
            to_cols.reshape(-1),
        ]
    ).astype(jnp.int32)

    arrived = contribute(
        child_panel[0], child_update[0], my_rows, my_cols, (cubes, rows, cols, row_cap, col_cap)
    )
    layout = (range_rows, range_cols, row_cap, col_cap)
    strip, pivot = assemble(tables, arrived, parent_front, layout)
    strip, lower, high, small, low = factor(strip, pivot, (cubes, rows, cols), layout)
    return final(tables, parent_front, strip, lower, high, small, low, arrived, layout)


def solution(mesh):
    placed = (P("cube", "row", "col"), P("cube", "row", None), P("row", ("cube", "col")), P())
    return jax.shard_map(
        body,
        mesh=mesh,
        in_specs=placed,
        out_specs=(P("row", ("cube", "col")), P("row", None)),
        check_vma=False,
    )
```

```python
import functools
import math

import jax
import jax.numpy as jnp
from jax import lax
from jax.experimental import pallas as pl
from jax.experimental.pallas import tpu as pltpu
from jax.sharding import PartitionSpec as P

BLK = 128
PANEL = 512
PB = PANEL // BLK
PAIR = 2 * BLK
SCALE_ROWS = 16
TOP = 32700.0
STEPS_PER_E = 64.0 / math.log(2.0)
HIGHEST = lax.Precision.HIGHEST
MESH = pl.DeviceIdType.MESH
ANY = pl.BlockSpec(memory_space=pl.ANY)
VMEM = pl.BlockSpec(memory_space=pltpu.VMEM)
SMEM = pl.BlockSpec(memory_space=pltpu.SMEM)


def group_ranks(labels):
    position = jnp.arange(labels.shape[-1])
    before = position[:, None] > position[None, :]
    same_label = labels[..., :, None] == labels[..., None, :]
    return jnp.sum(jnp.logical_and(same_label, before), axis=-1)


def member_of_slot(slot, slots, count):
    hits = (slot[:, None] == jnp.arange(slots)).astype(jnp.int32)
    return jnp.sum(hits * jnp.arange(count, dtype=jnp.int32)[:, None], axis=0)


def slot_of_block(grouped, slot_in_group, cap, first, count):
    groups = grouped.shape[1]
    wanted = first + jnp.arange(count, dtype=jnp.int32)
    hits = grouped[..., None] == wanted
    value = jnp.arange(groups, dtype=jnp.int32)[None, :, None] * cap + slot_in_group
    total = jnp.sum(jnp.where(hits, value[..., None] + 1, 0), axis=(1, 2))
    return total.astype(jnp.int32) - 1


def encode(x):
    peak = jnp.max(jnp.abs(x), axis=0, keepdims=True)
    unit = jnp.ceil(jnp.log(jnp.maximum(peak, 1e-30) * (1.0 / TOP)) * STEPS_PER_E)
    codes = jnp.round(x * jnp.exp(unit * (-1.0 / STEPS_PER_E)))
    return codes.astype(jnp.int32).astype(jnp.int16), unit


def scale_tile(units):
    width = units[0].shape[-1]
    row = lax.broadcasted_iota(jnp.int32, (SCALE_ROWS, width), 0)
    tile = jnp.zeros((SCALE_ROWS, width), jnp.float32)
    for index, unit in enumerate(units):
        tile = jnp.where(row == index, unit, tile)
    return tile.astype(jnp.int32).astype(jnp.int16)


def decode(codes, scales, index):
    scales = scales.astype(jnp.int32).astype(jnp.float32)
    row = lax.broadcasted_iota(jnp.int32, scales.shape, 0)
    unit = jnp.sum(jnp.where(row == index, scales, 0.0), axis=0, keepdims=True)
    return codes.astype(jnp.int32).astype(jnp.float32) * jnp.exp(unit * (1.0 / STEPS_PER_E))


def ring_position(index, count):
    odd = index % 2
    return (1 - odd) * (index // 2) + odd * (count - 1 - index // 2)


def ring_member(position, count):
    position = (position + count) % count
    back = position // (count // 2)
    return (1 - back) * (2 * position) + back * (2 * (count - 1 - position) + 1)


def greet_all(sizes):
    cubes, rows, cols = sizes
    count = cubes * rows * cols
    me = (lax.axis_index("cube") * rows + lax.axis_index("row")) * cols + lax.axis_index("col")
    barrier = pltpu.get_barrier_semaphore()

    def greet(step, carry):
        other = (me + step) % count
        device = (other // (rows * cols), (other // cols) % rows, other % cols)
        pl.semaphore_signal(barrier, inc=1, device_id=device, device_id_type=MESH)
        return carry

    lax.fori_loop(1, count, greet, 0)
    pl.semaphore_wait(barrier, count - 1)
    return me


def send(src, dst, send_sem, recv_sem, device):
    return pltpu.make_async_remote_copy(
        src_ref=src,
        dst_ref=dst,
        send_sem=send_sem,
        recv_sem=recv_sem,
        device_id=device,
        device_id_type=MESH,
    )


def pair_at(time, pairs, col):
    return ((pairs - 1) * time + col + 3) % pairs


def contribute_kernel(
    sizes, tables, own_any, update_any, arrived, own, column, update, product, packed,
    load_sem, pass_send, pass_recv, out_send, out_recv, keep_sem,
):
    cubes, rows, cols, row_cap, col_cap = sizes
    cube, row, col = lax.axis_index("cube"), lax.axis_index("row"), lax.axis_index("col")
    slots = cubes * cols * col_cap
    pairs = slots // 2
    together = min(2, col_cap)
    group_blocks = own.shape[0]
    col_blocks = update.shape[0]
    tile = min(PB, group_blocks)

    def load_update(block):
        left = pl.multiple_of(block * BLK, BLK)
        return pltpu.make_async_copy(
            update_any.at[:, :, pl.ds(left, BLK)], update.at[block], load_sem.at[1 + block]
        )

    load_own = pltpu.make_async_copy(own_any, own, load_sem.at[0])
    load_own.start()

    def start_load(block, carry):
        load_update(block).start()
        return carry

    lax.fori_loop(0, col_blocks, start_load, 0)
    me = greet_all((cubes, rows, cols))
    load_own.wait()

    place = ring_position(row, rows)
    forward_dist = (place - ring_position(col, rows) + rows) % rows
    dists = (forward_dist, (rows - forward_dist) % rows)
    nexts = (ring_member(place + 1, rows), ring_member(place - 1, rows))

    @pl.when(row == col)
    def _():
        def fill(slot, carry):
            column[slot] = own[tables[group_blocks + slot]]
            return carry

        lax.fori_loop(0, slots, fill, 0)

    def passing(slot, way):
        return send(
            column.at[slot],
            column.at[slot],
            pass_send.at[slot],
            pass_recv.at[slot],
            (cube, nexts[way], col),
        )

    def destination(slot, other_row):
        target = slot // col_cap
        return (target // cols, other_row, target % cols)

    def outgoing(slot, other_row):
        return send(
            packed.at[pl.ds(slot, together), other_row],
            arrived.at[cube, row, col, pl.ds(slot % col_cap, together)],
            out_send.at[slot // together, other_row],
            out_recv.at[me, (slot % col_cap) // together],
            destination(slot, other_row),
        )

    def staying(slot, other_row):
        return pltpu.make_async_copy(
            packed.at[pl.ds(slot, together), other_row],
            arrived.at[cube, row, col, pl.ds(slot % col_cap, together)],
            keep_sem.at[(slot % col_cap) // together],
        )

    def is_mine(slot, other_row):
        to_cube, to_row, to_col = destination(slot, other_row)
        return (to_cube == cube) & (to_row == row) & (to_col == col)

    def work(time):
        pair = pair_at(time, pairs, col)
        panel = column[pl.ds(2 * pair, 2)].reshape(PAIR, own.shape[2])

        def multiply(step, carry):
            at = pl.ds(step * tile, tile)
            product[at] = lax.dot_general(
                own[at].reshape(tile * BLK, own.shape[2]),
                panel,
                (((1,), (1,)), ((), ())),
                preferred_element_type=jnp.float32,
            ).reshape(tile, BLK, PAIR)
            return carry

        lax.fori_loop(0, group_blocks // tile, multiply, 0)

        def pack(step, carry):
            other_row = (row + 1 + step) % rows
            for half in range(2):
                slot = 2 * pair + half
                left = tables[group_blocks + slot]
                units = []
                for block in range(row_cap):
                    high = tables[other_row * row_cap + block]
                    value = update[left, high] - product[high, :, half * BLK : (half + 1) * BLK]
                    codes, unit = encode(value)
                    packed[slot, other_row, block * BLK : (block + 1) * BLK, :] = codes
                    units.append(unit)
                packed[slot, other_row, row_cap * BLK :, :] = scale_tile(units)
            for part in range(2 // together):
                slot = 2 * pair + part * together
                mine = is_mine(slot, other_row)

                @pl.when(mine)
                def _():
                    staying(slot, other_row).start()

                @pl.when(jnp.logical_not(mine))
                def _():
                    outgoing(slot, other_row).start()

            return carry

        lax.fori_loop(0, rows, pack, 0)

    def turn(time, carry):
        for way in range(2):
            step = time - dists[way]
            ready = (step >= 0) & (step < pairs)
            slot = 2 * pair_at(jnp.clip(step, 0, pairs - 1), pairs, col) + way

            @pl.when(ready & (dists[way] > 0))
            def _():
                passing(slot, way).wait_recv()

            @pl.when(ready & (dists[way] < rows - 1))
            def _():
                passing(slot, way).start()

        @pl.when(time == rows - 1)
        def _():
            def end_load(block, inner):
                load_update(block).wait()
                return inner

            lax.fori_loop(0, col_blocks, end_load, 0)

        @pl.when(time >= rows - 1)
        def _():
            work(jnp.maximum(time - (rows - 1), 0))

        return carry

    lax.fori_loop(0, pairs + rows - 1, turn, 0)

    for way in range(2):

        @pl.when(dists[way] < rows - 1)
        def _():
            def sent(pair, carry):
                passing(2 * pair + way, way).wait_send()
                return carry

            lax.fori_loop(0, pairs, sent, 0)

    def settle(index, carry):
        slot = (index // rows) * together
        other_row = index % rows
        mine = is_mine(slot, other_row)

        @pl.when(mine)
        def _():
            staying(slot, other_row).wait()

        @pl.when(jnp.logical_not(mine))
        def _():
            outgoing(slot, other_row).wait_send()

        return carry

    lax.fori_loop(0, (slots // together) * rows, settle, 0)

    count = cubes * rows * cols

    def collect(index, carry):
        other = (me + index) % count
        device = (other // (rows * cols), (other // cols) % rows, other % cols)
        for part in range(col_cap // together):
            send(
                packed.at[pl.ds(0, together), 0],
                arrived.at[
                    device[0], device[1], device[2], part * together : (part + 1) * together
                ],
                out_send.at[0, 0],
                out_recv.at[other, part],
                device,
            ).wait_recv()
        return carry

    lax.fori_loop(1, count, collect, 0)


def contribute(own_panel, update, my_rows, my_cols, sizes):
    cubes, rows, cols, row_cap, col_cap = sizes
    slots = cubes * cols * col_cap
    together = min(2, col_cap)
    depth = own_panel.shape[1]
    high, wide = update.shape[0] // BLK, update.shape[1] // BLK
    piece = row_cap * BLK + SCALE_ROWS
    tables = jnp.concatenate([my_rows, my_cols]).astype(jnp.int32)
    return pl.pallas_call(
        functools.partial(contribute_kernel, sizes),
        out_shape=jax.ShapeDtypeStruct((cubes, rows, cols, col_cap, piece, BLK), jnp.int16),
        in_specs=[SMEM, ANY, ANY],
        out_specs=ANY,
        scratch_shapes=[
            pltpu.VMEM((high, BLK, depth), own_panel.dtype),
            pltpu.VMEM((slots, BLK, depth), own_panel.dtype),
            pltpu.VMEM((wide, high, BLK, BLK), jnp.float32),
            pltpu.VMEM((high, BLK, PAIR), jnp.float32),
            pltpu.VMEM((slots, rows, piece, BLK), jnp.int16),
            pltpu.SemaphoreType.DMA((1 + wide,)),
            pltpu.SemaphoreType.DMA((slots,)),
            pltpu.SemaphoreType.DMA((slots,)),
            pltpu.SemaphoreType.DMA((slots // together, rows)),
            pltpu.SemaphoreType.DMA((cubes * rows * cols, col_cap // together)),
            pltpu.SemaphoreType.DMA((col_cap // together,)),
        ],
        compiler_params=pltpu.CompilerParams(
            collective_id=0, has_side_effects=True, vmem_limit_bytes=56 * 2**20
        ),
        name="contribute",
    )(tables, own_panel.reshape(high, BLK, depth), update.reshape(high, BLK, wide * BLK))


def arrivals(layout, tables, arrived, row_block, col_block):
    range_rows, range_cols, row_cap, col_cap = layout
    children = arrived.shape[0]
    found = []
    for child in range(children):
        row_slot = tables[child * range_rows + row_block]
        col_slot = tables[children * range_rows + child * range_cols + col_block]
        row_at, col_at = jnp.maximum(row_slot, 0), jnp.maximum(col_slot, 0)
        place = (child, row_at // row_cap, col_at // col_cap, col_at % col_cap)
        block = row_at % row_cap

        def piece(place=place, block=block):
            codes = arrived[place + (pl.ds(pl.multiple_of(block * BLK, BLK), BLK), slice(None))]
            scales = arrived[place + (pl.ds(row_cap * BLK, SCALE_ROWS), slice(None))]
            return decode(codes, scales, block)

        found.append(((row_slot >= 0) & (col_slot >= 0), piece))
    return found


def assemble_kernel(layout, tables, arrived, parent_any, strip_out, pivot_out, strip, total, sem):
    range_rows = layout[0]
    load = pltpu.make_async_copy(parent_any.at[:, pl.ds(0, PANEL)], strip, sem.at[0])
    load.start()
    load.wait()

    def strip_rows(step, carry):
        tile = jnp.zeros((SCALE_ROWS, PANEL), jnp.float32)
        for half in range(2):
            row_block = 2 * step + half
            high = pl.multiple_of(row_block * BLK, BLK)
            total[...] = strip[pl.ds(high, BLK), :].astype(jnp.float32)
            for block in range(PB):
                at = slice(block * BLK, (block + 1) * BLK)
                for valid, piece in arrivals(layout, tables, arrived, row_block, block):

                    @pl.when(valid)
                    def _(piece=piece):
                        total[:, at] += piece()

            codes, unit = encode(total[...])
            strip_out[step, half * BLK : (half + 1) * BLK, :] = codes
            row = lax.broadcasted_iota(jnp.int32, (SCALE_ROWS, PANEL), 0)
            tile = jnp.where(row == half, unit, tile)
            for block in range(PB):

                @pl.when(row_block == block)
                def _():
                    for other in range(block, PB):
                        pivot_out[block * PB + other] = total[:, other * BLK : (other + 1) * BLK]

        strip_out[step, PAIR:, :] = tile.astype(jnp.int32).astype(jnp.int16)
        return carry

    lax.fori_loop(0, range_rows // 2, strip_rows, 0)


def assemble(tables, arrived, parent, layout):
    range_rows = layout[0]
    return pl.pallas_call(
        functools.partial(assemble_kernel, layout),
        out_shape=(
            jax.ShapeDtypeStruct((range_rows // 2, PAIR + SCALE_ROWS, PANEL), jnp.int16),
            jax.ShapeDtypeStruct((PB * PB, BLK, BLK), jnp.float32),
        ),
        in_specs=[SMEM, VMEM, ANY],
        out_specs=(VMEM, VMEM),
        scratch_shapes=[
            pltpu.VMEM((range_rows * BLK, PANEL), parent.dtype),
            pltpu.VMEM((BLK, PANEL), jnp.float32),
            pltpu.SemaphoreType.DMA((1,)),
        ],
        compiler_params=pltpu.CompilerParams(vmem_limit_bytes=50 * 2**20),
        name="assemble",
    )(tables, arrived, parent)


SUB = 8
SUBS = BLK // SUB


def terms(x):
    first = x.astype(jnp.bfloat16).astype(jnp.float32)
    second = (x - first).astype(jnp.bfloat16).astype(jnp.float32)
    return first, second, x - first - second


def dot_full(a, b):
    a1, a2, a3 = terms(a)
    b1, b2, b3 = terms(b)
    left = jnp.concatenate([a1, a1, a2, a1, a2, a3], axis=0).astype(jnp.bfloat16)
    right = jnp.concatenate([b1, b2, b1, b3, b2, b1], axis=0).astype(jnp.bfloat16)
    return lax.dot_general(
        left, right, (((0,), (0,)), ((), ())), preferred_element_type=jnp.float32
    )


def eliminate_rows(step, diagonal):
    at = pl.ds(pl.multiple_of(step * SUB, SUB), SUB)
    block = diagonal[at, :]
    small = pltpu.roll(block[:, :BLK], (BLK - step * SUB) % BLK, 1)
    columns = [jnp.broadcast_to(small[:, j : j + 1], (SUB, BLK)) for j in range(SUB)]
    left = {
        (i, j): jnp.broadcast_to(columns[j][i : i + 1, :], (SUB, BLK))
        for j in range(SUB)
        for i in range(j, SUB)
    }
    done = [jnp.broadcast_to(block[i : i + 1, :], (SUB, 2 * BLK)) for i in range(SUB)]
    for k in range(SUB):
        pivot = left[k, k]
        root = lax.rsqrt(pivot)
        root = root * (1.5 - 0.5 * pivot * root * root)
        done[k] = done[k] * jnp.concatenate([root, root], axis=1)
        entries = {i: left[i, k] * root for i in range(k + 1, SUB)}
        for j in range(k + 1, SUB):
            for i in range(j, SUB):
                left[i, j] = left[i, j] - entries[i] * entries[j]
            wide = jnp.concatenate([entries[j], entries[j]], axis=1)
            done[j] = done[j] - wide * done[k]
    sub = lax.broadcasted_iota(jnp.int32, (SUB, 2 * BLK), 0)
    rows = done[0]
    for k in range(1, SUB):
        rows = jnp.where(sub == k, done[k], rows)
    diagonal[at, :] = rows
    lane = lax.broadcasted_iota(jnp.int32, (SUB, BLK), 1)
    below = jnp.where(lane >= (step + 1) * SUB, rows[:, :BLK], 0.0)
    diagonal[...] -= dot_full(below, rows)


def finish_block(block, whole, diagonal):
    at = pl.ds(pl.multiple_of(block * BLK, BLK), BLK)
    window = pl.ds(pl.multiple_of((block + 1) * BLK, BLK), PANEL)
    solved = jnp.dot(
        diagonal[:, BLK:], whole[at, window], precision=HIGHEST, preferred_element_type=jnp.float32
    )
    whole[at, at] = diagonal[:, :BLK]
    whole[at, window] = solved
    for below in range(1, PB):

        @pl.when(below > block)
        def _():
            whole[below * BLK : (below + 1) * BLK, window] -= dot_full(
                whole[at, below * BLK : (below + 1) * BLK], whole[at, window]
            )


def start_block(block, whole, diagonal):
    at = pl.ds(pl.multiple_of(block * BLK, BLK), BLK)
    diagonal[:, :BLK] = whole[at, at]
    eye = lax.broadcasted_iota(jnp.int32, (BLK, BLK), 0) == lax.broadcasted_iota(
        jnp.int32, (BLK, BLK), 1
    )
    diagonal[:, BLK:] = eye.astype(jnp.float32)


def split(x):
    high = x.astype(jnp.bfloat16)
    return high, (x - high.astype(jnp.float32)).astype(jnp.bfloat16)


def times_transposed(x, high, low):
    x_high, x_low = split(x)

    def product(a, b):
        return lax.dot_general(
            a, b, (((1,), (1,)), ((), ())), preferred_element_type=jnp.float32
        )

    return product(x_high, high) + (product(x_high, low) + product(x_low, high))


def decode_rows(chunk):
    scales = chunk[PAIR:, :]
    return jnp.concatenate(
        [decode(chunk[b * BLK : (b + 1) * BLK, :], scales, b) for b in range(2)], axis=0
    )


def factor_kernel(
    sizes, layout, strip_in, pivot_any, strip_all,
    lower_out, high_out, small_out, low_out,
    near, pivot, whole, diagonal, load_sem, pivot_send, pivot_recv, near_send, near_recv, near_keep,
    strip_send, strip_recv,
):
    cubes, rows, cols = sizes
    range_rows, range_cols = layout[:2]
    cube, row, col = lax.axis_index("cube"), lax.axis_index("row"), lax.axis_index("col")
    strips, nears = strip_all.shape[0], near.shape[0]
    upper = [i * PB + j for i in range(PB) for j in range(i, PB)]
    root = (cube == 0) & (row == 0) & (col == 0)

    @pl.when(root)
    def _():
        load = pltpu.make_async_copy(pivot_any, pivot, load_sem.at[0])
        load.start()
        load.wait()

    greet_all(sizes)

    place = ring_position(row, rows)
    half = rows // 2
    ahead, behind = ring_member(place + 1, rows), ring_member(place - 1, rows)
    back = (place + rows - 1) % rows
    children = [
        ((cube == 0) & (row == 0) & (col < cols - 1), (0, 0, col + 1)),
        ((cube == 0) & (place < half), (0, ahead, col)),
        ((cube == 0) & ((place == 0) | (place > half)) & (back > half), (0, behind, col)),
    ] + [(cube == 0, (other, row, col)) for other in range(1, cubes)]

    def pivot_copy(block, child):
        return send(
            pivot.at[block],
            pivot.at[block],
            pivot_send.at[block, child],
            pivot_recv.at[block],
            children[child][1],
        )

    near_ring = jnp.minimum(place, rows - place)
    depth = col + near_ring + jnp.where(cube > 0, 1, 0)
    batch = 4
    pivot_turns = -(-len(upper) // batch) + (cols - 1) + rows // 2 + 1

    def pass_pivot(blocks):
        for block in blocks:

            @pl.when(jnp.logical_not(root))
            def _():
                pivot_copy(block, 0).wait_recv()

            for child, (active, _) in enumerate(children):

                @pl.when(active)
                def _():
                    pivot_copy(block, child).start()

    def set_whole():
        whole[...] = jnp.zeros_like(whole)
        for i in range(PB):
            for j in range(i, PB):
                whole[i * BLK : (i + 1) * BLK, j * BLK : (j + 1) * BLK] = pivot[i * PB + j]
            eye = lax.broadcasted_iota(jnp.int32, (BLK, BLK), 0) == lax.broadcasted_iota(
                jnp.int32, (BLK, BLK), 1
            )
            whole[i * BLK : (i + 1) * BLK, PANEL + i * BLK : PANEL + (i + 1) * BLK] = eye.astype(
                jnp.float32
            )

    first = (cube * cols + col) * range_cols
    owner_place = ring_position(first // range_rows, rows)
    first_chunk = (first % range_rows) // 2
    sections = strips // nears
    section = first_chunk // nears
    ring_dist = (place - owner_place + rows) % rows
    dists = (ring_dist, (rows - ring_dist) % rows)
    nexts = (ahead, behind)
    owner = ring_dist == 0

    def near_copy(index, way, at_owner):
        return send(
            strip_all.at[first_chunk + index] if at_owner else near.at[index],
            near.at[index],
            near_send.at[index],
            near_recv.at[index],
            (cube, nexts[way], col),
        )

    def near_stay(index):
        return pltpu.make_async_copy(
            strip_all.at[first_chunk + index], near.at[index], near_keep.at[index]
        )

    strip_active = [(cube == 0) & (col < cols - 1)] + [cube == 0] * (cubes - 1)
    strip_got = (cube > 0) | (col > 0)

    def strip_copy(index, child):
        device = (0, row, col + 1) if child == 0 else (child, row, col)
        return send(
            strip_all.at[index], strip_all.at[index], strip_send.at[index, child],
            strip_recv.at[index], device,
        )

    turns = strips + cols + 2 * rows
    each = -(-PB * SUBS // (turns - pivot_turns))

    def turn(time, carry):
        for first_block in range(0, len(upper), batch):

            @pl.when(time == depth + first_block // batch)
            def _():
                pass_pivot(upper[first_block : first_block + batch])

        @pl.when(time == pivot_turns)
        def _():
            set_whole()

        lag = col + jnp.where(cube > 0, 1, 0)
        index = time - lag
        ready = (index >= 0) & (index < strips)
        index = jnp.clip(index, 0, strips - 1)
        index = (index % sections) * nears + index // sections

        @pl.when(ready & strip_got)
        def _():
            strip_copy(index, 0).wait_recv()

        for child, active in enumerate(strip_active):

            @pl.when(ready & active)
            def _():
                strip_copy(index, child).start()

        for way in range(2):
            step = time - lag - section - 2 * dists[way]
            late = jnp.clip(step, 0, strips - 1)
            chunk = late // sections
            due = (step >= 0) & (step < strips) & (late % sections == 0) & (chunk % 2 == way)

            @pl.when(due & jnp.logical_not(owner))
            def _():
                near_copy(chunk, way, False).wait_recv()

            @pl.when(due & jnp.logical_not(owner) & (dists[way] < rows - 1))
            def _():
                near_copy(chunk, way, False).start()

            @pl.when(due & owner)
            def _():
                near_copy(chunk, way, True).start()
                near_stay(chunk).start()

        def advance(sub, inner):
            step = (time - pivot_turns) * each + sub
            block = step // SUBS

            @pl.when((step >= 0) & (step < PB * SUBS))
            def _():
                @pl.when(step % SUBS == 0)
                def _():
                    start_block(block, whole, diagonal)

                eliminate_rows(step % SUBS, diagonal)

                @pl.when(step % SUBS == SUBS - 1)
                def _():
                    finish_block(block, whole, diagonal)

            return inner

        lax.fori_loop(0, each, advance, 0)
        return carry

    lax.fori_loop(0, turns, turn, 0)

    high_out[...], small_out[...] = split(whole[:, PANEL:])
    lower_out[...] = jnp.zeros_like(lower_out)
    for i in range(PB):
        for j in range(i + 1):
            block = whole[j * BLK : (j + 1) * BLK, i * BLK : (i + 1) * BLK].T
            if i == j:
                keep = lax.broadcasted_iota(jnp.int32, (BLK, BLK), 0) >= lax.broadcasted_iota(
                    jnp.int32, (BLK, BLK), 1
                )
                block = jnp.where(keep, block, 0.0)
            lower_out[i * BLK : (i + 1) * BLK, j * BLK : (j + 1) * BLK] = block

    @pl.when(owner)
    def _():
        def kept(index, carry):
            near_stay(index).wait()
            return carry

        lax.fori_loop(0, nears, kept, 0)

    def solve(index, carry):
        solved = times_transposed(decode_rows(near.at[index]), high_out[...], small_out[...])
        low_out[pl.ds(pl.multiple_of(index * PAIR, PAIR), PAIR), :] = solved.astype(low_out.dtype)
        return carry

    lax.fori_loop(0, nears, solve, 0)

    for block in upper:
        for child, (active, _) in enumerate(children):

            @pl.when(active)
            def _():
                pivot_copy(block, child).wait_send()

    def strips_sent(index, carry):
        for child, active in enumerate(strip_active):

            @pl.when(active)
            def _():
                strip_copy(index, child).wait_send()

        return carry

    lax.fori_loop(0, strips, strips_sent, 0)

    def nears_sent(index, carry):
        for way in range(2):

            @pl.when((index % 2 == way) & owner)
            def _():
                near_copy(index, way, True).wait_send()

            @pl.when((index % 2 == way) & jnp.logical_not(owner) & (dists[way] < rows - 1))
            def _():
                near_copy(index, way, False).wait_send()

        return carry

    lax.fori_loop(0, nears, nears_sent, 0)


def factor(strip, pivot, sizes, layout):
    cubes = sizes[0]
    range_cols = layout[1]
    square = (PANEL, PANEL)
    nears = range_cols // 2
    return pl.pallas_call(
        functools.partial(factor_kernel, sizes, layout),
        out_shape=(
            jax.ShapeDtypeStruct(strip.shape, strip.dtype),
            jax.ShapeDtypeStruct(square, jnp.float32),
            jax.ShapeDtypeStruct(square, jnp.bfloat16),
            jax.ShapeDtypeStruct(square, jnp.bfloat16),
            jax.ShapeDtypeStruct((range_cols * BLK, PANEL), jnp.bfloat16),
        ),
        in_specs=[ANY, ANY],
        out_specs=(ANY, VMEM, VMEM, VMEM, VMEM),
        input_output_aliases={0: 0},
        scratch_shapes=[
            pltpu.VMEM((nears,) + strip.shape[1:], strip.dtype),
            pltpu.VMEM(pivot.shape, pivot.dtype),
            pltpu.VMEM((PANEL, 2 * PANEL), jnp.float32),
            pltpu.VMEM((BLK, 2 * BLK), jnp.float32),
            pltpu.SemaphoreType.DMA((1,)),
            pltpu.SemaphoreType.DMA((PB * PB, 2 + cubes)),
            pltpu.SemaphoreType.DMA((PB * PB,)),
            pltpu.SemaphoreType.DMA((nears,)),
            pltpu.SemaphoreType.DMA((nears,)),
            pltpu.SemaphoreType.DMA((nears,)),
            pltpu.SemaphoreType.DMA((strip.shape[0], cubes)),
            pltpu.SemaphoreType.DMA((strip.shape[0],)),
        ],
        compiler_params=pltpu.CompilerParams(
            collective_id=1, has_side_effects=True, vmem_limit_bytes=50 * 2**20
        ),
        name="factor",
    )(strip, pivot)


def final_kernel(
    layout, tables, parent, strip, lower, high, small, low, arrived, schur, panel, solved, units
):
    range_rows, range_cols, row_cap, col_cap = layout
    children, groups, others = arrived.shape[:3]
    step = pl.program_id(0)
    base = children * (range_rows + range_cols)
    first_row, first_col = tables[base], tables[base + 1]

    @pl.when(step == 0)
    def _():
        def read(index, carry):
            at = (index // (groups * others), (index // others) % groups, index % others)
            for rank in range(col_cap):
                scales = arrived[at + (rank, slice(row_cap * BLK, None), slice(None))]
                scales = scales.astype(jnp.int32).astype(jnp.float32)
                units[at + (rank,)] = jnp.exp(scales * (1.0 / STEPS_PER_E))
            return carry

        lax.fori_loop(0, children * groups * others, read, 0)

    solved[...] = times_transposed(decode_rows(strip.at[0]), high[...], small[...])

    @pl.when(first_row + 2 * step < PB)
    def _():
        solved[...] = lower[...]

    panel[...] = solved[...]
    left = solved[...].astype(jnp.bfloat16)
    for chunk in range(range_cols // PB):
        at = slice(chunk * PANEL, (chunk + 1) * PANEL)
        product = lax.dot_general(
            left, low[at, :], (((1,), (1,)), ((), ())), preferred_element_type=jnp.float32
        )
        keep = first_row + 2 * step >= PB
        if chunk == 0:
            keep = keep & (first_col >= PB)
        schur[:, at] = jnp.where(keep, parent[:, at].astype(jnp.float32) - product, 0.0)
    for half in range(2):
        row_block = 2 * step + half
        rows = slice(half * BLK, (half + 1) * BLK)
        for child in range(children):
            row_slot = tables[child * range_rows + row_block]

            @pl.when((row_slot >= 0) & (first_row + row_block >= PB))
            def _():
                group, block = row_slot // row_cap, row_slot % row_cap
                high_at = pl.ds(pl.multiple_of(block * BLK, BLK), BLK)
                for slot in range(others * col_cap):
                    place = (child, group, slot // col_cap, slot % col_cap)
                    to = tables[base + 2 + child * others * col_cap + slot]
                    wanted = (to >= 0) & (first_col + to >= PB)
                    at = pl.ds(pl.multiple_of(jnp.maximum(to, 0) * BLK, BLK), BLK)
                    unit = units[place + (pl.ds(block, 1), slice(None))]
                    unit = unit * jnp.where(wanted, 1.0, 0.0)
                    codes = arrived[place + (high_at, slice(None))]
                    schur[rows, at] += codes.astype(jnp.int32).astype(jnp.float32) * unit


def final(tables, parent, strip, lower, high, small, low, arrived, layout):
    height, width = parent.shape
    return pl.pallas_call(
        functools.partial(final_kernel, layout),
        out_shape=(
            jax.ShapeDtypeStruct((height, width), jnp.float32),
            jax.ShapeDtypeStruct((height, PANEL), jnp.float32),
        ),
        grid_spec=pltpu.PrefetchScalarGridSpec(
            num_scalar_prefetch=1,
            grid=(height // PAIR,),
            in_specs=[
                pl.BlockSpec((PAIR, width), lambda s, t: (s, 0)),
                pl.BlockSpec((1,) + strip.shape[1:], lambda s, t: (s, 0, 0)),
                pl.BlockSpec((PAIR, PANEL), lambda s, t: (jnp.minimum(s, PANEL // PAIR - 1), 0)),
                VMEM,
                VMEM,
                VMEM,
                VMEM,
            ],
            out_specs=(
                pl.BlockSpec((PAIR, width), lambda s, t: (s, 0)),
                pl.BlockSpec((PAIR, PANEL), lambda s, t: (s, 0)),
            ),
            scratch_shapes=[
                pltpu.VMEM((PAIR, PANEL), jnp.float32),
                pltpu.VMEM(arrived.shape[:4] + (SCALE_ROWS, BLK), jnp.float32),
            ],
        ),
        compiler_params=pltpu.CompilerParams(vmem_limit_bytes=50 * 2**20),
        name="final",
    )(tables, parent, strip, lower, high, small, low, arrived)


def body(child_update, child_panel, parent_front, block_map):
    rows = lax.axis_size("row")
    cubes = lax.axis_size("cube")
    cols = lax.axis_size("col")
    ranges = cubes * cols
    child_index = lax.axis_index("cube")
    row_index = lax.axis_index("row")
    col_index = lax.axis_index("col")
    range_index = lax.axis_index(("cube", "col"))
    group_blocks = child_update.shape[1] // BLK
    row_cap = group_blocks // rows
    col_cap = max(1, group_blocks // ranges)
    range_rows = parent_front.shape[0] // BLK
    range_cols = parent_front.shape[1] // BLK

    children = block_map.shape[0]
    grouped = block_map.reshape(children, rows, group_blocks)
    row_dest = grouped // range_rows
    col_dest = grouped // range_cols
    row_slot = row_dest * row_cap + group_ranks(row_dest)
    col_rank = group_ranks(col_dest)
    row_rank = row_slot - row_dest * row_cap
    col_slot = col_dest * col_cap + col_rank
    my_rows = member_of_slot(row_slot[child_index, row_index], group_blocks, group_blocks)
    my_cols = member_of_slot(col_slot[child_index, col_index], ranges * col_cap, group_blocks)
    from_rows = slot_of_block(grouped, row_rank, row_cap, row_index * range_rows, range_rows)
    from_cols = slot_of_block(grouped, col_rank, col_cap, range_index * range_cols, range_cols)
    local = grouped - range_index * range_cols
    inside = (local >= 0) & (local < range_cols)
    at_rank = col_rank[..., None] == jnp.arange(col_cap)
    to_cols = jnp.sum(jnp.where(inside[..., None] & at_rank, local[..., None] + 1, 0), axis=2) - 1
    tables = jnp.concatenate(
        [
            from_rows.reshape(-1),
            from_cols.reshape(-1),
            jnp.stack([row_index * range_rows, range_index * range_cols]),
            to_cols.reshape(-1),
        ]
    ).astype(jnp.int32)

    arrived = contribute(
        child_panel[0], child_update[0], my_rows, my_cols, (cubes, rows, cols, row_cap, col_cap)
    )
    layout = (range_rows, range_cols, row_cap, col_cap)
    strip, pivot = assemble(tables, arrived, parent_front, layout)
    strip, lower, high, small, low = factor(strip, pivot, (cubes, rows, cols), layout)
    return final(tables, parent_front, strip, lower, high, small, low, arrived, layout)


def solution(mesh):
    placed = (P("cube", "row", "col"), P("cube", "row", None), P("row", ("cube", "col")), P())
    return jax.shard_map(
        body,
        mesh=mesh,
        in_specs=placed,
        out_specs=(P("row", ("cube", "col")), P("row", None)),
        check_vma=False,
    )
```

```python
import functools
import math

import jax
import jax.numpy as jnp
from jax import lax
from jax.experimental import pallas as pl
from jax.experimental.pallas import tpu as pltpu
from jax.sharding import PartitionSpec as P

BLK = 128
PANEL = 512
PB = PANEL // BLK
PAIR = 2 * BLK
SCALE_ROWS = 16
TOP = 32700.0
STEPS_PER_E = 64.0 / math.log(2.0)
HIGHEST = lax.Precision.HIGHEST
MESH = pl.DeviceIdType.MESH
ANY = pl.BlockSpec(memory_space=pl.ANY)
VMEM = pl.BlockSpec(memory_space=pltpu.VMEM)
SMEM = pl.BlockSpec(memory_space=pltpu.SMEM)


def group_ranks(labels):
    position = jnp.arange(labels.shape[-1])
    before = position[:, None] > position[None, :]
    same_label = labels[..., :, None] == labels[..., None, :]
    return jnp.sum(jnp.logical_and(same_label, before), axis=-1)


def member_of_slot(slot, slots, count):
    hits = (slot[:, None] == jnp.arange(slots)).astype(jnp.int32)
    return jnp.sum(hits * jnp.arange(count, dtype=jnp.int32)[:, None], axis=0)


def slot_of_block(grouped, slot_in_group, cap, first, count):
    groups = grouped.shape[1]
    wanted = first + jnp.arange(count, dtype=jnp.int32)
    hits = grouped[..., None] == wanted
    value = jnp.arange(groups, dtype=jnp.int32)[None, :, None] * cap + slot_in_group
    total = jnp.sum(jnp.where(hits, value[..., None] + 1, 0), axis=(1, 2))
    return total.astype(jnp.int32) - 1


def encode(x):
    peak = jnp.max(jnp.abs(x), axis=0, keepdims=True)
    unit = jnp.ceil(jnp.log(jnp.maximum(peak, 1e-30) * (1.0 / TOP)) * STEPS_PER_E)
    codes = jnp.round(x * jnp.exp(unit * (-1.0 / STEPS_PER_E)))
    return codes.astype(jnp.int32).astype(jnp.int16), unit


def scale_tile(units):
    width = units[0].shape[-1]
    row = lax.broadcasted_iota(jnp.int32, (SCALE_ROWS, width), 0)
    tile = jnp.zeros((SCALE_ROWS, width), jnp.float32)
    for index, unit in enumerate(units):
        tile = jnp.where(row == index, unit, tile)
    return tile.astype(jnp.int32).astype(jnp.int16)


def decode(codes, scales, index):
    scales = scales.astype(jnp.int32).astype(jnp.float32)
    row = lax.broadcasted_iota(jnp.int32, scales.shape, 0)
    unit = jnp.sum(jnp.where(row == index, scales, 0.0), axis=0, keepdims=True)
    return codes.astype(jnp.int32).astype(jnp.float32) * jnp.exp(unit * (1.0 / STEPS_PER_E))


def ring_position(index, count):
    odd = index % 2
    return (1 - odd) * (index // 2) + odd * (count - 1 - index // 2)


def ring_member(position, count):
    position = (position + count) % count
    back = position // (count // 2)
    return (1 - back) * (2 * position) + back * (2 * (count - 1 - position) + 1)


def greet_all(sizes):
    cubes, rows, cols = sizes
    count = cubes * rows * cols
    me = (lax.axis_index("cube") * rows + lax.axis_index("row")) * cols + lax.axis_index("col")
    barrier = pltpu.get_barrier_semaphore()

    def greet(step, carry):
        other = (me + step) % count
        device = (other // (rows * cols), (other // cols) % rows, other % cols)
        pl.semaphore_signal(barrier, inc=1, device_id=device, device_id_type=MESH)
        return carry

    lax.fori_loop(1, count, greet, 0)
    pl.semaphore_wait(barrier, count - 1)
    return me


def send(src, dst, send_sem, recv_sem, device):
    return pltpu.make_async_remote_copy(
        src_ref=src,
        dst_ref=dst,
        send_sem=send_sem,
        recv_sem=recv_sem,
        device_id=device,
        device_id_type=MESH,
    )


def pair_at(time, pairs, col):
    return ((pairs - 1) * time + col + 3) % pairs


def contribute_kernel(
    sizes, tables, own_any, update_any, arrived, own, column, update, product, packed,
    load_sem, pass_send, pass_recv, out_send, out_recv, keep_sem,
):
    cubes, rows, cols, row_cap, col_cap = sizes
    cube, row, col = lax.axis_index("cube"), lax.axis_index("row"), lax.axis_index("col")
    slots = cubes * cols * col_cap
    pairs = slots // 2
    together = min(2, col_cap)
    group_blocks = own.shape[0]
    col_blocks = update.shape[0]
    tile = min(PB, group_blocks)

    def load_update(block):
        left = pl.multiple_of(block * BLK, BLK)
        return pltpu.make_async_copy(
            update_any.at[:, :, pl.ds(left, BLK)], update.at[block], load_sem.at[1 + block]
        )

    load_own = pltpu.make_async_copy(own_any, own, load_sem.at[0])
    load_own.start()

    def start_load(block, carry):
        load_update(block).start()
        return carry

    lax.fori_loop(0, col_blocks, start_load, 0)
    me = greet_all((cubes, rows, cols))
    load_own.wait()

    place = ring_position(row, rows)
    forward_dist = (place - ring_position(col, rows) + rows) % rows
    dists = (forward_dist, (rows - forward_dist) % rows)
    nexts = (ring_member(place + 1, rows), ring_member(place - 1, rows))

    @pl.when(row == col)
    def _():
        def fill(slot, carry):
            column[slot] = own[tables[group_blocks + slot]]
            return carry

        lax.fori_loop(0, slots, fill, 0)

    def passing(slot, way):
        return send(
            column.at[slot],
            column.at[slot],
            pass_send.at[slot],
            pass_recv.at[slot],
            (cube, nexts[way], col),
        )

    def destination(slot, other_row):
        target = slot // col_cap
        return (target // cols, other_row, target % cols)

    def outgoing(slot, other_row):
        return send(
            packed.at[pl.ds(slot, together), other_row],
            arrived.at[cube, row, col, pl.ds(slot % col_cap, together)],
            out_send.at[slot // together, other_row],
            out_recv.at[me, (slot % col_cap) // together],
            destination(slot, other_row),
        )

    def staying(slot, other_row):
        return pltpu.make_async_copy(
            packed.at[pl.ds(slot, together), other_row],
            arrived.at[cube, row, col, pl.ds(slot % col_cap, together)],
            keep_sem.at[(slot % col_cap) // together],
        )

    def is_mine(slot, other_row):
        to_cube, to_row, to_col = destination(slot, other_row)
        return (to_cube == cube) & (to_row == row) & (to_col == col)

    def work(time):
        pair = pair_at(time, pairs, col)
        panel = column[pl.ds(2 * pair, 2)].reshape(PAIR, own.shape[2])

        def multiply(step, carry):
            at = pl.ds(step * tile, tile)
            product[at] = lax.dot_general(
                own[at].reshape(tile * BLK, own.shape[2]),
                panel,
                (((1,), (1,)), ((), ())),
                preferred_element_type=jnp.float32,
            ).reshape(tile, BLK, PAIR)
            return carry

        lax.fori_loop(0, group_blocks // tile, multiply, 0)

        def pack(step, carry):
            other_row = (row + 1 + step) % rows
            for half in range(2):
                slot = 2 * pair + half
                left = tables[group_blocks + slot]
                units = []
                for block in range(row_cap):
                    high = tables[other_row * row_cap + block]
                    value = update[left, high] - product[high, :, half * BLK : (half + 1) * BLK]
                    codes, unit = encode(value)
                    packed[slot, other_row, block * BLK : (block + 1) * BLK, :] = codes
                    units.append(unit)
                packed[slot, other_row, row_cap * BLK :, :] = scale_tile(units)
            for part in range(2 // together):
                slot = 2 * pair + part * together
                mine = is_mine(slot, other_row)

                @pl.when(mine)
                def _():
                    staying(slot, other_row).start()

                @pl.when(jnp.logical_not(mine))
                def _():
                    outgoing(slot, other_row).start()

            return carry

        lax.fori_loop(0, rows, pack, 0)

    def turn(time, carry):
        for way in range(2):
            step = time - dists[way]
            ready = (step >= 0) & (step < pairs)
            slot = 2 * pair_at(jnp.clip(step, 0, pairs - 1), pairs, col) + way

            @pl.when(ready & (dists[way] > 0))
            def _():
                passing(slot, way).wait_recv()

            @pl.when(ready & (dists[way] < rows - 1))
            def _():
                passing(slot, way).start()

        @pl.when(time == rows - 1)
        def _():
            def end_load(block, inner):
                load_update(block).wait()
                return inner

            lax.fori_loop(0, col_blocks, end_load, 0)

        @pl.when(time >= rows - 1)
        def _():
            work(jnp.maximum(time - (rows - 1), 0))

        return carry

    lax.fori_loop(0, pairs + rows - 1, turn, 0)

    for way in range(2):

        @pl.when(dists[way] < rows - 1)
        def _():
            def sent(pair, carry):
                passing(2 * pair + way, way).wait_send()
                return carry

            lax.fori_loop(0, pairs, sent, 0)

    def settle(index, carry):
        slot = (index // rows) * together
        other_row = index % rows
        mine = is_mine(slot, other_row)

        @pl.when(mine)
        def _():
            staying(slot, other_row).wait()

        @pl.when(jnp.logical_not(mine))
        def _():
            outgoing(slot, other_row).wait_send()

        return carry

    lax.fori_loop(0, (slots // together) * rows, settle, 0)

    count = cubes * rows * cols

    def collect(index, carry):
        other = (me + index) % count
        device = (other // (rows * cols), (other // cols) % rows, other % cols)
        for part in range(col_cap // together):
            send(
                packed.at[pl.ds(0, together), 0],
                arrived.at[
                    device[0], device[1], device[2], part * together : (part + 1) * together
                ],
                out_send.at[0, 0],
                out_recv.at[other, part],
                device,
            ).wait_recv()
        return carry

    lax.fori_loop(1, count, collect, 0)


def contribute(own_panel, update, my_rows, my_cols, sizes):
    cubes, rows, cols, row_cap, col_cap = sizes
    slots = cubes * cols * col_cap
    together = min(2, col_cap)
    depth = own_panel.shape[1]
    high, wide = update.shape[0] // BLK, update.shape[1] // BLK
    piece = row_cap * BLK + SCALE_ROWS
    tables = jnp.concatenate([my_rows, my_cols]).astype(jnp.int32)
    return pl.pallas_call(
        functools.partial(contribute_kernel, sizes),
        out_shape=jax.ShapeDtypeStruct((cubes, rows, cols, col_cap, piece, BLK), jnp.int16),
        in_specs=[SMEM, ANY, ANY],
        out_specs=ANY,
        scratch_shapes=[
            pltpu.VMEM((high, BLK, depth), own_panel.dtype),
            pltpu.VMEM((slots, BLK, depth), own_panel.dtype),
            pltpu.VMEM((wide, high, BLK, BLK), jnp.float32),
            pltpu.VMEM((high, BLK, PAIR), jnp.float32),
            pltpu.VMEM((slots, rows, piece, BLK), jnp.int16),
            pltpu.SemaphoreType.DMA((1 + wide,)),
            pltpu.SemaphoreType.DMA((slots,)),
            pltpu.SemaphoreType.DMA((slots,)),
            pltpu.SemaphoreType.DMA((slots // together, rows)),
            pltpu.SemaphoreType.DMA((cubes * rows * cols, col_cap // together)),
            pltpu.SemaphoreType.DMA((col_cap // together,)),
        ],
        compiler_params=pltpu.CompilerParams(
            collective_id=0, has_side_effects=True, vmem_limit_bytes=56 * 2**20
        ),
        name="contribute",
    )(tables, own_panel.reshape(high, BLK, depth), update.reshape(high, BLK, wide * BLK))


def arrivals(layout, tables, arrived, row_block, col_block):
    range_rows, range_cols, row_cap, col_cap = layout
    children = arrived.shape[0]
    found = []
    for child in range(children):
        row_slot = tables[child * range_rows + row_block]
        col_slot = tables[children * range_rows + child * range_cols + col_block]
        row_at, col_at = jnp.maximum(row_slot, 0), jnp.maximum(col_slot, 0)
        place = (child, row_at // row_cap, col_at // col_cap, col_at % col_cap)
        block = row_at % row_cap

        def piece(place=place, block=block):
            codes = arrived[place + (pl.ds(pl.multiple_of(block * BLK, BLK), BLK), slice(None))]
            scales = arrived[place + (pl.ds(row_cap * BLK, SCALE_ROWS), slice(None))]
            return decode(codes, scales, block)

        found.append(((row_slot >= 0) & (col_slot >= 0), piece))
    return found


def assemble_kernel(layout, tables, arrived, parent_any, strip_out, pivot_out, strip, total, sem):
    range_rows = layout[0]
    load = pltpu.make_async_copy(parent_any.at[:, pl.ds(0, PANEL)], strip, sem.at[0])
    load.start()
    load.wait()

    def strip_rows(step, carry):
        tile = jnp.zeros((SCALE_ROWS, PANEL), jnp.float32)
        for half in range(2):
            row_block = 2 * step + half
            high = pl.multiple_of(row_block * BLK, BLK)
            total[...] = strip[pl.ds(high, BLK), :].astype(jnp.float32)
            for block in range(PB):
                at = slice(block * BLK, (block + 1) * BLK)
                for valid, piece in arrivals(layout, tables, arrived, row_block, block):

                    @pl.when(valid)
                    def _(piece=piece):
                        total[:, at] += piece()

            codes, unit = encode(total[...])
            strip_out[step, half * BLK : (half + 1) * BLK, :] = codes
            row = lax.broadcasted_iota(jnp.int32, (SCALE_ROWS, PANEL), 0)
            tile = jnp.where(row == half, unit, tile)
            for block in range(PB):

                @pl.when(row_block == block)
                def _():
                    for other in range(block, PB):
                        pivot_out[block * PB + other] = total[:, other * BLK : (other + 1) * BLK]

        strip_out[step, PAIR:, :] = tile.astype(jnp.int32).astype(jnp.int16)
        return carry

    lax.fori_loop(0, range_rows // 2, strip_rows, 0)


def assemble(tables, arrived, parent, layout):
    range_rows = layout[0]
    return pl.pallas_call(
        functools.partial(assemble_kernel, layout),
        out_shape=(
            jax.ShapeDtypeStruct((range_rows // 2, PAIR + SCALE_ROWS, PANEL), jnp.int16),
            jax.ShapeDtypeStruct((PB * PB, BLK, BLK), jnp.float32),
        ),
        in_specs=[SMEM, VMEM, ANY],
        out_specs=(VMEM, VMEM),
        scratch_shapes=[
            pltpu.VMEM((range_rows * BLK, PANEL), parent.dtype),
            pltpu.VMEM((BLK, PANEL), jnp.float32),
            pltpu.SemaphoreType.DMA((1,)),
        ],
        compiler_params=pltpu.CompilerParams(vmem_limit_bytes=50 * 2**20),
        name="assemble",
    )(tables, arrived, parent)


SUB = 8
SUBS = BLK // SUB


def terms(x):
    first = x.astype(jnp.bfloat16).astype(jnp.float32)
    second = (x - first).astype(jnp.bfloat16).astype(jnp.float32)
    return first, second, x - first - second


def dot_full(a, b):
    a1, a2, a3 = terms(a)
    b1, b2, b3 = terms(b)
    left = jnp.concatenate([a1, a1, a2, a1, a2, a3], axis=0).astype(jnp.bfloat16)
    right = jnp.concatenate([b1, b2, b1, b3, b2, b1], axis=0).astype(jnp.bfloat16)
    return lax.dot_general(
        left, right, (((0,), (0,)), ((), ())), preferred_element_type=jnp.float32
    )


def eliminate_rows(step, diagonal):
    at = pl.ds(pl.multiple_of(step * SUB, SUB), SUB)
    block = diagonal[at, :]
    small = pltpu.roll(block[:, :BLK], (BLK - step * SUB) % BLK, 1)
    columns = [jnp.broadcast_to(small[:, j : j + 1], (SUB, BLK)) for j in range(SUB)]
    left = {
        (i, j): jnp.broadcast_to(columns[j][i : i + 1, :], (SUB, BLK))
        for j in range(SUB)
        for i in range(j, SUB)
    }
    done = [jnp.broadcast_to(block[i : i + 1, :], (SUB, 2 * BLK)) for i in range(SUB)]
    for k in range(SUB):
        pivot = left[k, k]
        root = lax.rsqrt(pivot)
        root = root * (1.5 - 0.5 * pivot * root * root)
        done[k] = done[k] * jnp.concatenate([root, root], axis=1)
        entries = {i: left[i, k] * root for i in range(k + 1, SUB)}
        for j in range(k + 1, SUB):
            for i in range(j, SUB):
                left[i, j] = left[i, j] - entries[i] * entries[j]
            wide = jnp.concatenate([entries[j], entries[j]], axis=1)
            done[j] = done[j] - wide * done[k]
    sub = lax.broadcasted_iota(jnp.int32, (SUB, 2 * BLK), 0)
    rows = done[0]
    for k in range(1, SUB):
        rows = jnp.where(sub == k, done[k], rows)
    diagonal[at, :] = rows
    lane = lax.broadcasted_iota(jnp.int32, (SUB, BLK), 1)
    below = jnp.where(lane >= (step + 1) * SUB, rows[:, :BLK], 0.0)
    diagonal[...] -= dot_full(below, rows)


def finish_block(block, whole, diagonal):
    at = pl.ds(pl.multiple_of(block * BLK, BLK), BLK)
    window = pl.ds(pl.multiple_of((block + 1) * BLK, BLK), PANEL)
    solved = jnp.dot(
        diagonal[:, BLK:], whole[at, window], precision=HIGHEST, preferred_element_type=jnp.float32
    )
    whole[at, at] = diagonal[:, :BLK]
    whole[at, window] = solved
    for below in range(1, PB):

        @pl.when(below > block)
        def _():
            whole[below * BLK : (below + 1) * BLK, window] -= dot_full(
                whole[at, below * BLK : (below + 1) * BLK], whole[at, window]
            )


def start_block(block, whole, diagonal):
    at = pl.ds(pl.multiple_of(block * BLK, BLK), BLK)
    diagonal[:, :BLK] = whole[at, at]
    eye = lax.broadcasted_iota(jnp.int32, (BLK, BLK), 0) == lax.broadcasted_iota(
        jnp.int32, (BLK, BLK), 1
    )
    diagonal[:, BLK:] = eye.astype(jnp.float32)


def split(x):
    high = x.astype(jnp.bfloat16)
    return high, (x - high.astype(jnp.float32)).astype(jnp.bfloat16)


def times_transposed(x, high, low):
    x_high, x_low = split(x)

    def product(a, b):
        return lax.dot_general(
            a, b, (((1,), (1,)), ((), ())), preferred_element_type=jnp.float32
        )

    return product(x_high, high) + (product(x_high, low) + product(x_low, high))


def decode_rows(chunk):
    scales = chunk[PAIR:, :]
    return jnp.concatenate(
        [decode(chunk[b * BLK : (b + 1) * BLK, :], scales, b) for b in range(2)], axis=0
    )


def factor_kernel(
    sizes, layout, strip_in, pivot_any, strip_all,
    lower_out, high_out, small_out, low_out,
    near, pivot, whole, diagonal, load_sem, pivot_send, pivot_recv, near_send, near_recv, near_keep,
    strip_send, strip_recv,
):
    cubes, rows, cols = sizes
    range_rows, range_cols = layout[:2]
    cube, row, col = lax.axis_index("cube"), lax.axis_index("row"), lax.axis_index("col")
    strips, nears = strip_all.shape[0], near.shape[0]
    upper = [i * PB + j for i in range(PB) for j in range(i, PB)]
    root = (cube == 0) & (row == 0) & (col == 0)

    @pl.when(root)
    def _():
        load = pltpu.make_async_copy(pivot_any, pivot, load_sem.at[0])
        load.start()
        load.wait()

    greet_all(sizes)

    place = ring_position(row, rows)
    half = rows // 2
    ahead, behind = ring_member(place + 1, rows), ring_member(place - 1, rows)
    back = (place + rows - 1) % rows
    children = [
        ((cube == 0) & (row == 0) & (col < cols - 1), (0, 0, col + 1)),
        ((cube == 0) & (place < half), (0, ahead, col)),
        ((cube == 0) & ((place == 0) | (place > half)) & (back > half), (0, behind, col)),
    ] + [(cube == 0, (other, row, col)) for other in range(1, cubes)]

    def pivot_copy(block, child):
        return send(
            pivot.at[block],
            pivot.at[block],
            pivot_send.at[block, child],
            pivot_recv.at[block],
            children[child][1],
        )

    near_ring = jnp.minimum(place, rows - place)
    depth = col + near_ring + jnp.where(cube > 0, 1, 0)
    batch = 4
    pivot_turns = -(-len(upper) // batch) + (cols - 1) + rows // 2 + 1

    def pass_pivot(blocks):
        for block in blocks:

            @pl.when(jnp.logical_not(root))
            def _():
                pivot_copy(block, 0).wait_recv()

            for child, (active, _) in enumerate(children):

                @pl.when(active)
                def _():
                    pivot_copy(block, child).start()

    def set_whole():
        whole[...] = jnp.zeros_like(whole)
        for i in range(PB):
            for j in range(i, PB):
                whole[i * BLK : (i + 1) * BLK, j * BLK : (j + 1) * BLK] = pivot[i * PB + j]
            eye = lax.broadcasted_iota(jnp.int32, (BLK, BLK), 0) == lax.broadcasted_iota(
                jnp.int32, (BLK, BLK), 1
            )
            whole[i * BLK : (i + 1) * BLK, PANEL + i * BLK : PANEL + (i + 1) * BLK] = eye.astype(
                jnp.float32
            )

    first = (cube * cols + col) * range_cols
    owner_place = ring_position(first // range_rows, rows)
    first_chunk = (first % range_rows) // 2
    sections = strips // nears
    section = first_chunk // nears
    ring_dist = (place - owner_place + rows) % rows
    dists = (ring_dist, (rows - ring_dist) % rows)
    nexts = (ahead, behind)
    owner = ring_dist == 0

    def near_copy(index, way, at_owner):
        return send(
            strip_all.at[first_chunk + index] if at_owner else near.at[index],
            near.at[index],
            near_send.at[index],
            near_recv.at[index],
            (cube, nexts[way], col),
        )

    def near_stay(index):
        return pltpu.make_async_copy(
            strip_all.at[first_chunk + index], near.at[index], near_keep.at[index]
        )

    strip_active = [(cube == 0) & (col < cols - 1)] + [cube == 0] * (cubes - 1)
    strip_got = (cube > 0) | (col > 0)

    def strip_copy(index, child):
        device = (0, row, col + 1) if child == 0 else (child, row, col)
        return send(
            strip_all.at[index], strip_all.at[index], strip_send.at[index, child],
            strip_recv.at[index], device,
        )

    turns = strips + cols + 3 * rows
    each = -(-PB * SUBS // (turns - pivot_turns))

    def turn(time, carry):
        for first_block in range(0, len(upper), batch):

            @pl.when(time == depth + first_block // batch)
            def _():
                pass_pivot(upper[first_block : first_block + batch])

        @pl.when(time == pivot_turns)
        def _():
            set_whole()

        lag = col + jnp.where(cube > 0, 1, 0)
        index = time - lag
        ready = (index >= 0) & (index < strips)
        index = jnp.clip(index, 0, strips - 1)
        index = (index % sections) * nears + index // sections

        @pl.when(ready & strip_got)
        def _():
            strip_copy(index, 0).wait_recv()

        for child, active in enumerate(strip_active):

            @pl.when(ready & active)
            def _():
                strip_copy(index, child).start()

        for way in range(2):
            step = time - lag - section - 3 * dists[way]
            late = jnp.clip(step, 0, strips - 1)
            chunk = late // sections
            due = (step >= 0) & (step < strips) & (late % sections == 0) & (chunk % 2 == way)

            @pl.when(due & jnp.logical_not(owner))
            def _():
                near_copy(chunk, way, False).wait_recv()

            @pl.when(due & jnp.logical_not(owner) & (dists[way] < rows - 1))
            def _():
                near_copy(chunk, way, False).start()

            @pl.when(due & owner)
            def _():
                near_copy(chunk, way, True).start()
                near_stay(chunk).start()

        def advance(sub, inner):
            step = (time - pivot_turns) * each + sub
            block = step // SUBS

            @pl.when((step >= 0) & (step < PB * SUBS))
            def _():
                @pl.when(step % SUBS == 0)
                def _():
                    start_block(block, whole, diagonal)

                eliminate_rows(step % SUBS, diagonal)

                @pl.when(step % SUBS == SUBS - 1)
                def _():
                    finish_block(block, whole, diagonal)

            return inner

        lax.fori_loop(0, each, advance, 0)
        return carry

    lax.fori_loop(0, turns, turn, 0)

    high_out[...], small_out[...] = split(whole[:, PANEL:])
    lower_out[...] = jnp.zeros_like(lower_out)
    for i in range(PB):
        for j in range(i + 1):
            block = whole[j * BLK : (j + 1) * BLK, i * BLK : (i + 1) * BLK].T
            if i == j:
                keep = lax.broadcasted_iota(jnp.int32, (BLK, BLK), 0) >= lax.broadcasted_iota(
                    jnp.int32, (BLK, BLK), 1
                )
                block = jnp.where(keep, block, 0.0)
            lower_out[i * BLK : (i + 1) * BLK, j * BLK : (j + 1) * BLK] = block

    @pl.when(owner)
    def _():
        def kept(index, carry):
            near_stay(index).wait()
            return carry

        lax.fori_loop(0, nears, kept, 0)

    def solve(index, carry):
        solved = times_transposed(decode_rows(near.at[index]), high_out[...], small_out[...])
        low_out[pl.ds(pl.multiple_of(index * PAIR, PAIR), PAIR), :] = solved.astype(low_out.dtype)
        return carry

    lax.fori_loop(0, nears, solve, 0)

    for block in upper:
        for child, (active, _) in enumerate(children):

            @pl.when(active)
            def _():
                pivot_copy(block, child).wait_send()

    def strips_sent(index, carry):
        for child, active in enumerate(strip_active):

            @pl.when(active)
            def _():
                strip_copy(index, child).wait_send()

        return carry

    lax.fori_loop(0, strips, strips_sent, 0)

    def nears_sent(index, carry):
        for way in range(2):

            @pl.when((index % 2 == way) & owner)
            def _():
                near_copy(index, way, True).wait_send()

            @pl.when((index % 2 == way) & jnp.logical_not(owner) & (dists[way] < rows - 1))
            def _():
                near_copy(index, way, False).wait_send()

        return carry

    lax.fori_loop(0, nears, nears_sent, 0)


def factor(strip, pivot, sizes, layout):
    cubes = sizes[0]
    range_cols = layout[1]
    square = (PANEL, PANEL)
    nears = range_cols // 2
    return pl.pallas_call(
        functools.partial(factor_kernel, sizes, layout),
        out_shape=(
            jax.ShapeDtypeStruct(strip.shape, strip.dtype),
            jax.ShapeDtypeStruct(square, jnp.float32),
            jax.ShapeDtypeStruct(square, jnp.bfloat16),
            jax.ShapeDtypeStruct(square, jnp.bfloat16),
            jax.ShapeDtypeStruct((range_cols * BLK, PANEL), jnp.bfloat16),
        ),
        in_specs=[ANY, ANY],
        out_specs=(ANY, VMEM, VMEM, VMEM, VMEM),
        input_output_aliases={0: 0},
        scratch_shapes=[
            pltpu.VMEM((nears,) + strip.shape[1:], strip.dtype),
            pltpu.VMEM(pivot.shape, pivot.dtype),
            pltpu.VMEM((PANEL, 2 * PANEL), jnp.float32),
            pltpu.VMEM((BLK, 2 * BLK), jnp.float32),
            pltpu.SemaphoreType.DMA((1,)),
            pltpu.SemaphoreType.DMA((PB * PB, 2 + cubes)),
            pltpu.SemaphoreType.DMA((PB * PB,)),
            pltpu.SemaphoreType.DMA((nears,)),
            pltpu.SemaphoreType.DMA((nears,)),
            pltpu.SemaphoreType.DMA((nears,)),
            pltpu.SemaphoreType.DMA((strip.shape[0], cubes)),
            pltpu.SemaphoreType.DMA((strip.shape[0],)),
        ],
        compiler_params=pltpu.CompilerParams(
            collective_id=1, has_side_effects=True, vmem_limit_bytes=50 * 2**20
        ),
        name="factor",
    )(strip, pivot)


def final_kernel(
    layout, tables, parent, strip, lower, high, small, low, arrived, schur, panel, solved, units
):
    range_rows, range_cols, row_cap, col_cap = layout
    children, groups, others = arrived.shape[:3]
    step = pl.program_id(0)
    base = children * (range_rows + range_cols)
    first_row, first_col = tables[base], tables[base + 1]

    @pl.when(step == 0)
    def _():
        def read(index, carry):
            at = (index // (groups * others), (index // others) % groups, index % others)
            for rank in range(col_cap):
                scales = arrived[at + (rank, slice(row_cap * BLK, None), slice(None))]
                scales = scales.astype(jnp.int32).astype(jnp.float32)
                units[at + (rank,)] = jnp.exp(scales * (1.0 / STEPS_PER_E))
            return carry

        lax.fori_loop(0, children * groups * others, read, 0)

    solved[...] = times_transposed(decode_rows(strip.at[0]), high[...], small[...])

    @pl.when(first_row + 2 * step < PB)
    def _():
        solved[...] = lower[...]

    panel[...] = solved[...]
    left = solved[...].astype(jnp.bfloat16)
    for chunk in range(range_cols // PB):
        at = slice(chunk * PANEL, (chunk + 1) * PANEL)
        product = lax.dot_general(
            left, low[at, :], (((1,), (1,)), ((), ())), preferred_element_type=jnp.float32
        )
        keep = first_row + 2 * step >= PB
        if chunk == 0:
            keep = keep & (first_col >= PB)
        schur[:, at] = jnp.where(keep, parent[:, at].astype(jnp.float32) - product, 0.0)
    for half in range(2):
        row_block = 2 * step + half
        rows = slice(half * BLK, (half + 1) * BLK)
        for child in range(children):
            row_slot = tables[child * range_rows + row_block]

            @pl.when((row_slot >= 0) & (first_row + row_block >= PB))
            def _():
                group, block = row_slot // row_cap, row_slot % row_cap
                high_at = pl.ds(pl.multiple_of(block * BLK, BLK), BLK)
                for slot in range(others * col_cap):
                    place = (child, group, slot // col_cap, slot % col_cap)
                    to = tables[base + 2 + child * others * col_cap + slot]
                    wanted = (to >= 0) & (first_col + to >= PB)
                    at = pl.ds(pl.multiple_of(jnp.maximum(to, 0) * BLK, BLK), BLK)
                    unit = units[place + (pl.ds(block, 1), slice(None))]
                    unit = unit * jnp.where(wanted, 1.0, 0.0)
                    codes = arrived[place + (high_at, slice(None))]
                    schur[rows, at] += codes.astype(jnp.int32).astype(jnp.float32) * unit


def final(tables, parent, strip, lower, high, small, low, arrived, layout):
    height, width = parent.shape
    return pl.pallas_call(
        functools.partial(final_kernel, layout),
        out_shape=(
            jax.ShapeDtypeStruct((height, width), jnp.float32),
            jax.ShapeDtypeStruct((height, PANEL), jnp.float32),
        ),
        grid_spec=pltpu.PrefetchScalarGridSpec(
            num_scalar_prefetch=1,
            grid=(height // PAIR,),
            in_specs=[
                pl.BlockSpec((PAIR, width), lambda s, t: (s, 0)),
                pl.BlockSpec((1,) + strip.shape[1:], lambda s, t: (s, 0, 0)),
                pl.BlockSpec((PAIR, PANEL), lambda s, t: (jnp.minimum(s, PANEL // PAIR - 1), 0)),
                VMEM,
                VMEM,
                VMEM,
                VMEM,
            ],
            out_specs=(
                pl.BlockSpec((PAIR, width), lambda s, t: (s, 0)),
                pl.BlockSpec((PAIR, PANEL), lambda s, t: (s, 0)),
            ),
            scratch_shapes=[
                pltpu.VMEM((PAIR, PANEL), jnp.float32),
                pltpu.VMEM(arrived.shape[:4] + (SCALE_ROWS, BLK), jnp.float32),
            ],
        ),
        compiler_params=pltpu.CompilerParams(vmem_limit_bytes=50 * 2**20),
        name="final",
    )(tables, parent, strip, lower, high, small, low, arrived)


def body(child_update, child_panel, parent_front, block_map):
    rows = lax.axis_size("row")
    cubes = lax.axis_size("cube")
    cols = lax.axis_size("col")
    ranges = cubes * cols
    child_index = lax.axis_index("cube")
    row_index = lax.axis_index("row")
    col_index = lax.axis_index("col")
    range_index = lax.axis_index(("cube", "col"))
    group_blocks = child_update.shape[1] // BLK
    row_cap = group_blocks // rows
    col_cap = max(1, group_blocks // ranges)
    range_rows = parent_front.shape[0] // BLK
    range_cols = parent_front.shape[1] // BLK

    children = block_map.shape[0]
    grouped = block_map.reshape(children, rows, group_blocks)
    row_dest = grouped // range_rows
    col_dest = grouped // range_cols
    row_slot = row_dest * row_cap + group_ranks(row_dest)
    col_rank = group_ranks(col_dest)
    row_rank = row_slot - row_dest * row_cap
    col_slot = col_dest * col_cap + col_rank
    my_rows = member_of_slot(row_slot[child_index, row_index], group_blocks, group_blocks)
    my_cols = member_of_slot(col_slot[child_index, col_index], ranges * col_cap, group_blocks)
    from_rows = slot_of_block(grouped, row_rank, row_cap, row_index * range_rows, range_rows)
    from_cols = slot_of_block(grouped, col_rank, col_cap, range_index * range_cols, range_cols)
    local = grouped - range_index * range_cols
    inside = (local >= 0) & (local < range_cols)
    at_rank = col_rank[..., None] == jnp.arange(col_cap)
    to_cols = jnp.sum(jnp.where(inside[..., None] & at_rank, local[..., None] + 1, 0), axis=2) - 1
    tables = jnp.concatenate(
        [
            from_rows.reshape(-1),
            from_cols.reshape(-1),
            jnp.stack([row_index * range_rows, range_index * range_cols]),
            to_cols.reshape(-1),
        ]
    ).astype(jnp.int32)

    arrived = contribute(
        child_panel[0], child_update[0], my_rows, my_cols, (cubes, rows, cols, row_cap, col_cap)
    )
    layout = (range_rows, range_cols, row_cap, col_cap)
    strip, pivot = assemble(tables, arrived, parent_front, layout)
    strip, lower, high, small, low = factor(strip, pivot, (cubes, rows, cols), layout)
    return final(tables, parent_front, strip, lower, high, small, low, arrived, layout)


def solution(mesh):
    placed = (P("cube", "row", "col"), P("cube", "row", None), P("row", ("cube", "col")), P())
    return jax.shard_map(
        body,
        mesh=mesh,
        in_specs=placed,
        out_specs=(P("row", ("cube", "col")), P("row", None)),
        check_vma=False,
    )
```
